32 devices in a mesh: heads: 2 (over core), tokens: 16 (over z, y, x).
Axes of the slice: x: 2, y: 2, z: 4, core: 2. Of those that a mesh axis runs over, the one named last changes fastest.
Arguments:
- queries: bfloat16 [2, 2048, 2048], P(None, 'tokens', 'heads'), may hold values from -8.5 to 8.5, as said below
- keys: bfloat16 [2, 2048, 2048], P(None, 'tokens', 'heads'), may hold values from -6 to 6
- values: bfloat16 [2, 2048, 2048], P(None, 'tokens', 'heads'), may hold values from -6 to 6
- rates: float32 [2, 8, 2048], P(None, 'heads', 'tokens'), may hold values from 0.05 to 1
- fast_init: bfloat16 [8, 3, 256, 256], P('heads'), may hold values from -0.375 to 0.375
- out_gain: float32 [2048], P('heads'), may hold values from 0.25 to 1.75
Outputs:
- mixed: bfloat16 [2, 2048, 2048], P(None, 'tokens', 'heads')
- final_weights: bfloat16 [8, 3, 256, 256], P('heads')
The draws below stay inside these ranges and needn't reach their ends.
Inputs may be any that keep to these rules, and one draw needn't show every extreme that they name: queries are real-valued and of order one.
All inputs are finite; a program needn't handle non-finite values.
Results may differ from the reference program's by a relative error of at most 0.0095.
Values may be sent and summed in bfloat16 or wider, within the bound.
A program may use at most 64 MiB of HBM per device.

```python
import math
import jax
import jax.numpy as jnp
from jax import lax

HEADS = 8
DH = 256
D = 2048
GROUPS = 2
NS_STEPS = 2
GROUP = 2048


def draw_queries(key, part):
    first = jax.random.fold_in(jax.random.fold_in(key, 11), 0)
    column_head = jnp.arange(D) // DH
    scale = 0.6 + 0.8 * column_head.astype(jnp.float32) / (HEADS - 1)
    base = jnp.clip(jax.random.normal(first, (GROUPS, GROUP, D), jnp.float32), -6.0, 6.0)
    return (base * scale[None, None, :]).astype(jnp.bfloat16)


def steps_of(own_key, dims, cuts, low, high):
    def one(position, shards_of):
        heights = jax.random.uniform(jax.random.fold_in(jax.random.fold_in(own_key, 6), position), (shards_of,), jnp.float32, low / len(cuts), high / len(cuts))
        return jnp.repeat(jnp.exp(heights), dims[position] // shards_of).reshape((-1,) + (1,) * (len(dims) - position - 1))

    loudness = one(*cuts[0])
    for cut in cuts[1:]:
        loudness = loudness * one(*cut)
    return loudness


def bell_draw(stream_key, extent, spread, bound, pieces=(), kind=jnp.bfloat16):
    drawn = spread * jax.random.normal(stream_key, extent, jnp.float32)
    if pieces:
        drawn = drawn * steps_of(stream_key, extent, pieces, -0.22, 0.18)
    return jnp.clip(drawn, -bound, bound).astype(kind)


def setup_inputs(seed: int = 0) -> dict:
    splits = jax.random.split(jax.random.key(seed), 7)
    return {
        "queries": draw_queries(jax.random.fold_in(splits[6], 71), 0),
        "keys": bell_draw(splits[1], (GROUPS, GROUP, D), 1.0, 6.0, ((1, 16), (2, 2))),
        "values": bell_draw(splits[2], (GROUPS, GROUP, D), 1.0, 6.0, ((1, 16), (2, 2))),
        "rates": jnp.clip(jnp.exp(math.log(1.0) - 2.9957323 * jax.random.uniform(splits[3], (GROUPS, HEADS, GROUP), jnp.float32) ** steps_of(splits[3], (GROUPS, HEADS, GROUP), ((1, 2), (2, 16)), -0.2, 0.2)), 0.05, 1.0),
        "fast_init": bell_draw(splits[4], (HEADS, 3, DH, DH), DH ** -0.5, 0.375, ((0, 2),)),
        "out_gain": jnp.clip(1.0 + 0.15 * jax.random.normal(splits[5], (D,), jnp.float32), 0.25, 1.75),
    }


coef_a = 3.4445
coef_b = -4.775
coef_c = 2.0315
step_size = 0.5

def newton(grads):
    squares = lax.optimization_barrier(jnp.sum(grads * grads, axis=(1, 2)))
    current = (grads / (jnp.sqrt(squares)[:, None, None] + 1e-07)).astype(jnp.bfloat16)
    for step in range(NS_STEPS):
        wide = current.astype(jnp.float32)
        gram = jnp.einsum('mij,mkj->mik', wide, wide).astype(jnp.bfloat16)
        gram_wide = gram.astype(jnp.float32)
        square = jnp.einsum('mij,mjk->mik', gram_wide, gram_wide)
        mixer = (coef_b * gram_wide + coef_c * square).astype(jnp.bfloat16)
        current = (coef_a * wide + jnp.einsum('mij,mjk->mik', mixer.astype(jnp.float32), wide)).astype(jnp.bfloat16)
    return current

def head_step(items):
    query, key_rows, value_rows, rate, weight = items
    gate_q = jnp.dot(query, weight[0], preferred_element_type=jnp.float32)
    up_q = jnp.dot(query, weight[1], preferred_element_type=jnp.float32)
    hidden_q = (jax.nn.silu(gate_q) * up_q).astype(jnp.bfloat16)
    output = jnp.dot(hidden_q, weight[2], preferred_element_type=jnp.float32)
    gate_k = jnp.dot(key_rows, weight[0], preferred_element_type=jnp.float32)
    up_k = jnp.dot(key_rows, weight[1], preferred_element_type=jnp.float32)
    sig = jax.nn.sigmoid(gate_k)
    hidden = (gate_k * sig * up_k).astype(jnp.bfloat16)
    scaled = (rate[:, None] * value_rows.astype(jnp.float32)).astype(jnp.bfloat16)
    back = jnp.dot(scaled, weight[2].T, preferred_element_type=jnp.float32)
    grad_gate = (back * up_k * sig * (1.0 + gate_k * (1.0 - sig))).astype(jnp.bfloat16)
    grad_up = (back * gate_k * sig).astype(jnp.bfloat16)
    g_gate = jnp.dot(key_rows.T, grad_gate, preferred_element_type=jnp.float32)
    g_up = jnp.dot(key_rows.T, grad_up, preferred_element_type=jnp.float32)
    g_down = jnp.dot(hidden.T, scaled, preferred_element_type=jnp.float32)
    update = newton(jnp.stack([g_gate, g_up, g_down], axis=0))
    fresh = (weight.astype(jnp.float32) + step_size * update.astype(jnp.float32)).astype(jnp.bfloat16)
    return (output, fresh)

def reference(queries, keys, values, rates, fast_init, out_gain):
    weights = fast_init
    mixed = []
    for block in range(GROUPS):
        query = queries[block].reshape(GROUP, HEADS, DH).transpose(1, 0, 2)
        key_rows = keys[block].reshape(GROUP, HEADS, DH).transpose(1, 0, 2)
        value_rows = values[block].reshape(GROUP, HEADS, DH).transpose(1, 0, 2)
        outputs, weights = lax.map(head_step, (query, key_rows, value_rows, rates[block], weights))
        joined = outputs.transpose(1, 0, 2).reshape(GROUP, D)
        meansq = lax.optimization_barrier(jnp.mean(joined * joined, axis=1, keepdims=True))
        mixed.append((joined / jnp.sqrt(meansq + 1e-06) * out_gain[None, :]).astype(jnp.bfloat16))
    return (jnp.stack(mixed, axis=0), weights)
```

```python
import functools

import jax
import jax.numpy as jnp
from jax import lax
from jax.experimental import pallas as pl
from jax.experimental.pallas import tpu as pltpu
from jax.sharding import PartitionSpec as P

D = 2048
NS_STEPS = 2


coef_a = 3.4445
coef_b = -4.775
coef_c = 2.0315
step_size = 0.5


def newton(current):
    for step in range(NS_STEPS):
        gram = jnp.einsum(
            "hmij,hmkj->hmik", current, current, preferred_element_type=jnp.float32
        ).astype(jnp.bfloat16)
        square = jnp.einsum("hmij,hmjk->hmik", gram, gram, preferred_element_type=jnp.float32)
        mixer = (coef_b * gram.astype(jnp.float32) + coef_c * square).astype(jnp.bfloat16)
        product = jnp.einsum("hmij,hmjk->hmik", mixer, current, preferred_element_type=jnp.float32)
        current = (coef_a * current.astype(jnp.float32) + product).astype(jnp.bfloat16)
    return current


def apply_heads(query, weights):
    gate_q = jnp.einsum("nhd,hde->nhe", query, weights[:, 0], preferred_element_type=jnp.float32)
    up_q = jnp.einsum("nhd,hde->nhe", query, weights[:, 1], preferred_element_type=jnp.float32)
    hidden_q = (jax.nn.silu(gate_q) * up_q).astype(jnp.bfloat16)
    return jnp.einsum("nhd,hde->nhe", hidden_q, weights[:, 2], preferred_element_type=jnp.float32)


def local_grads(key_rows, value_rows, rate, weights):
    gate_k = jnp.einsum("nhd,hde->nhe", key_rows, weights[:, 0], preferred_element_type=jnp.float32)
    up_k = jnp.einsum("nhd,hde->nhe", key_rows, weights[:, 1], preferred_element_type=jnp.float32)
    sig = jax.nn.sigmoid(gate_k)
    hidden = (gate_k * sig * up_k).astype(jnp.bfloat16)
    scaled = (rate.T[:, :, None] * value_rows.astype(jnp.float32)).astype(jnp.bfloat16)
    back = jnp.einsum("nhe,hde->nhd", scaled, weights[:, 2], preferred_element_type=jnp.float32)
    grad_gate = (back * up_k * sig * (1.0 + gate_k * (1.0 - sig))).astype(jnp.bfloat16)
    grad_up = (back * gate_k * sig).astype(jnp.bfloat16)
    g_gate = jnp.einsum("nhd,nhe->hde", key_rows, grad_gate, preferred_element_type=jnp.float32)
    g_up = jnp.einsum("nhd,nhe->hde", key_rows, grad_up, preferred_element_type=jnp.float32)
    g_down = jnp.einsum("nhd,nhe->hde", hidden, scaled, preferred_element_type=jnp.float32)
    return jnp.stack([g_gate, g_up, g_down], axis=1)


def finish(joined, totals, out_gain):
    return (joined / jnp.sqrt(totals[:, None] / D + 1e-06) * out_gain[None, :]).astype(jnp.bfloat16)


def per_device(queries, keys, values, rates, fast_init, out_gain):
    heads_here = fast_init.shape[0]
    head_size = fast_init.shape[2]
    tok_rows = queries.shape[1]
    weights = fast_init
    outputs = []
    joined_all = []
    for block in range(queries.shape[0]):
        query = queries[block].reshape(tok_rows, heads_here, head_size)
        key_rows = keys[block].reshape(tok_rows, heads_here, head_size)
        value_rows = values[block].reshape(tok_rows, heads_here, head_size)
        joined = apply_heads(query, weights).reshape(tok_rows, heads_here * head_size)
        grads = local_grads(key_rows, value_rows, rates[block], weights)
        total = lax.psum(grads, "tokens")
        squares = jnp.sum(total * total, axis=(2, 3))
        start = (total / (jnp.sqrt(squares)[:, :, None, None] + 1e-07)).astype(jnp.bfloat16)
        update = newton(start)
        weights = (weights.astype(jnp.float32) + step_size * update.astype(jnp.float32)).astype(
            jnp.bfloat16
        )
        joined_all.append(joined)
    stacked = jnp.stack(joined_all, axis=0)
    totals = lax.psum(jnp.sum(stacked * stacked, axis=2), "heads")
    outputs = [
        finish(joined_all[index], totals[index], out_gain) for index in range(len(joined_all))
    ]
    return (jnp.stack(outputs, axis=0), weights)


F32 = jnp.float32
BF16 = jnp.bfloat16
MESH = pl.DeviceIdType.MESH
DOWN, GATE, UP = 2, 0, 1
ORDER = (DOWN, GATE, UP)


def mm(a, b):
    return jnp.dot(a, b, preferred_element_type=F32)


def mm_nt(a, b):
    return lax.dot_general(a, b, (((1,), (1,)), ((), ())), preferred_element_type=F32)


def mm_tn(a, b):
    return lax.dot_general(a, b, (((0,), (0,)), ((), ())), preferred_element_type=F32)


def orthogonalize(mats):
    xs = []
    for g in mats:
        g = g.astype(F32)
        square = jnp.sum(jnp.sum(g * g, axis=1, keepdims=True), axis=0, keepdims=True)
        xs.append((g / (jnp.sqrt(square) + 1e-07)).astype(BF16))
    for _ in range(NS_STEPS):
        grams = [mm_nt(x, x).astype(BF16) for x in xs]
        mixers = [(coef_b * a.astype(F32) + coef_c * mm(a, a)).astype(BF16) for a in grams]
        xs = [(coef_a * x.astype(F32) + mm(b, x)).astype(BF16) for b, x in zip(mixers, xs)]
    return xs


def kernel(
    sizes, q_hbm, k_hbm, v_hbm, r_hbm, w_hbm, gain_hbm, mixed, wout,
    q0, vals, w0, rates, gain, dps, kv, qb, act, dgu, hid, w_own, w1, wgu, gd_s, gd_r, gg_s, gg_r, full_d, full_g,
    ysend, ybuf, y0, sq, sqr,
    loc_sem, a2a_s, kv_r, q_r, w_sem, fwd_s, x_s, x_r, c_s, c_r, y_sem, sq_s, sq_r, dc_r, ds_r, dist_s,
):
    cores, HL, rows, DH = sizes
    width = HL * DH
    half = DH // 2
    core = lax.axis_index("heads")
    t = lax.axis_index("tokens")
    x, y, zl, zh = t % 2, (t // 2) % 2, (t // 4) % 2, t // 8
    z = t // 4
    kind = (y + zl) % 2
    home = core == kind
    away = core != kind
    away_bit = (core + kind) % 2
    home_bit = 1 - away_bit

    def pick(first, second):
        return jnp.where(kind == 0, first, second)

    def by_core(first, second):
        return jnp.where(core == 0, first, second)

    own_bits = (pick(x, y), pick(y, zl), pick(zl, zh))
    source_slot = by_core(x + 2 * y + 4 * zl, y + 2 * zl + 4 * zh)
    own_head = pick(x + 2 * zl, z)
    mate = pick(t + 8 * (1 - 2 * zh), t + 1 - 2 * x)
    x_near = t + 1 - 2 * x
    y_near = t + 2 * (1 - 2 * y)
    z_near = t + 4 * (1 - 2 * zl)

    def slot(k, flip=0):
        bits = (k % 2, (k // 2) % 2, k // 4 + flip)
        return sum(((own_bits[i] + bits[i]) % 2) * 2 ** i for i in range(3))

    def group_tokens(k, flip=0):
        a, b, c = k % 2, (k // 2) % 2, k // 4 + flip
        first = (x + a) % 2 + 2 * ((y + b) % 2) + 4 * ((zl + c) % 2) + 8 * zh
        second = x + 2 * ((y + a) % 2) + 4 * ((zl + b) % 2) + 8 * ((zh + c) % 2)
        return pick(first, second)

    def owner(j):
        return by_core(j % 2 + 6 * (j // 2) + 8 * zh, x + 2 * (1 - j % 2) + 4 * j)

    def remote(src, dst, send_sem, recv_sem, device):
        return pltpu.make_async_remote_copy(
            src_ref=src, dst_ref=dst, send_sem=send_sem, recv_sem=recv_sem,
            device_id=device, device_id_type=MESH,
        )

    def send(src, dst, send_sem, recv_sem, device):
        remote(src, dst, send_sem, recv_sem, device).start()

    def arrived(ref, recv_sem):
        remote(ref, ref, loc_sem.at[0], recv_sem, {"tokens": x_near}).wait_recv()

    def drained(ref, send_sem):
        remote(ref, ref, send_sem, loc_sem.at[0], {"tokens": x_near}).wait_send()

    def cols(h):
        return pl.ds(pl.multiple_of(h * DH, DH), DH)

    twin = {"heads": 1 - core}

    local_v = [pltpu.make_async_copy(v_hbm.at[b], vals.at[b], loc_sem.at[4 + b]) for b in range(2)]
    local_r = pltpu.make_async_copy(r_hbm, rates, loc_sem.at[2])
    local_q = pltpu.make_async_copy(q_hbm.at[0], q0, loc_sem.at[0])
    local_w = pltpu.make_async_copy(w_hbm, w0, loc_sem.at[1])
    local_gain = pltpu.make_async_copy(gain_hbm, gain, loc_sem.at[3])
    own_w = pltpu.make_async_copy(w_hbm.at[own_head], w_own, w_sem.at[0])
    local_r.start()
    local_v[0].start()
    local_w.start()
    local_q.start()
    local_v[1].start()
    local_gain.start()

    @pl.when(home)
    def _():
        own_w.start()

    barrier = pltpu.get_barrier_semaphore()

    @pl.when(away)
    def _():
        for k in range(8):
            pl.semaphore_signal(
                barrier, inc=1, device_id={"heads": 1 - core, "tokens": group_tokens(k)}, device_id_type=MESH
            )

    for device in ({"tokens": mate}, {"heads": 1 - core}, {"tokens": x_near}, {"tokens": y_near}):
        pl.semaphore_signal(barrier, inc=1, device_id=device, device_id_type=MESH)

    @pl.when(z < 3)
    def _():
        pl.semaphore_signal(barrier, inc=1, device_id={"tokens": t + 4}, device_id_type=MESH)

    @pl.when(z > 0)
    def _():
        pl.semaphore_signal(barrier, inc=1, device_id={"tokens": t - 4}, device_id_type=MESH)

    pl.semaphore_wait(barrier, HL + 4 + 1 + jnp.where((z == 0) | (z == 3), 0, 1))

    base = by_core(x + 2 * zl, z)

    def spread(array, view, landing, recv_sems):
        for k in SPREAD:
            j = (base + k) % HL
            send(view(j), landing.at[source_slot], a2a_s.at[array], recv_sems.at[source_slot],
                 {"heads": 1 - core, "tokens": owner(j)})

    def spread_keys(b):
        spread(2 * b, lambda j: k_hbm.at[b, :, cols(j)], kv.at[2 * b], kv_r.at[2 * b])

    def spread_values(b):
        spread(2 * b + 1, lambda j: dps.at[b, j], kv.at[2 * b + 1], kv_r.at[2 * b + 1])

    def spread_queries():
        spread(4, lambda j: q_hbm.at[1, :, cols(j)], qb, q_r)

    def scale_values(b):
        for j in range(HL):
            rate = jnp.broadcast_to(rates[b, pl.ds(j, 1), :], (rows, rows)).T[:, :1]
            dps[b, j] = (rate * vals[b, :, j * DH:(j + 1) * DH].astype(F32)).astype(BF16)

    spread_keys(0)

    @pl.when(home)
    def _():
        send(w_hbm.at[own_head], w_own, fwd_s.at[5], w_sem.at[0], twin)

    local_r.wait()
    local_v[0].wait()
    scale_values(0)
    spread_values(0)
    local_v[1].wait()
    scale_values(1)
    if EARLY >= 1:
        spread_keys(1)
    if EARLY >= 2:
        spread_values(1)
    if EARLY >= 3:
        spread_queries()

    def share_squares(b, square):
        sq[b] = jnp.broadcast_to(square, (rows, 128))
        send(sq.at[b], sqr.at[b], sq_s.at[b], sq_r.at[b], twin)

    def finish_block(b, read):
        total = sq[b]
        arrived(sqr.at[b], sq_r.at[b])
        total = total + sqr[b]
        root = jnp.sqrt(total[:, :1] / (cores * width) + 1e-06)
        for h in range(HL):
            span = slice(h * DH, (h + 1) * DH)
            mixed[b, :, span] = (read(h) / root * gain[:, span]).astype(BF16)

    def fast_net(rows_in, w_gate, w_up, w_down):
        gate = mm(rows_in, w_gate)
        hidden = (jax.nn.silu(gate) * mm(rows_in, w_up)).astype(BF16)
        return mm(hidden, w_down)

    local_w.wait()
    local_q.wait()
    square = jnp.zeros((rows, 1), F32)
    for h in range(HL):
        span = slice(h * DH, (h + 1) * DH)
        out = fast_net(q0[:, span], w0[h, 0], w0[h, 1], w0[h, 2])
        y0[:, span] = out
        square = square + jnp.sum(out * out, axis=1, keepdims=True)
    share_squares(0, square)

    def halve_weights(w):
        for c in range(2):
            span = slice(c * half, (c + 1) * half)
            wgu[c] = jnp.concatenate([w[GATE, :, span], w[UP, :, span]], axis=1)

    def forward(array, i, when):
        @pl.when(when)
        def _():
            send(kv.at[array, i], kv.at[array, i], fwd_s.at[array], kv_r.at[array, i], twin)

    def gradients(b, w):
        weights = wgu[core]
        w_down = w[DOWN, pl.ds(pl.multiple_of(core * half, half), half), :]
        for k in range(8):
            i = slot(k)
            if b == 0:
                arrived(kv.at[0, i], kv_r.at[0, i])
                forward(0, i, away)
            else:
                @pl.when(home)
                def _():
                    arrived(kv.at[2, i], kv_r.at[2, i])
            act[k] = mm(kv[2 * b, i], weights)
        for k in range(8):
            i = slot(k)
            if b == 0:
                arrived(kv.at[1, i], kv_r.at[1, i])
                forward(1, i, away)
            else:
                @pl.when(home)
                def _():
                    arrived(kv.at[3, i], kv_r.at[3, i])
            back = mm_nt(kv[2 * b + 1, i], w_down)
            gate = act[k, :, :half]
            up = act[k, :, half:]
            sig = jax.nn.sigmoid(gate)
            hid[i] = (gate * sig * up).astype(BF16)
            dgu[i, :, :half] = (back * up * sig * (1.0 + gate * (1.0 - sig))).astype(BF16)
            dgu[i, :, half:] = (back * gate * sig).astype(BF16)
        count = 8 * rows
        grad = mm_tn(hid[...].reshape(count, half), kv[2 * b + 1].reshape(count, DH))
        gd_s[b] = grad.astype(BF16)
        send(gd_s.at[b], gd_r.at[b], x_s.at[b], x_r.at[b, DOWN], {"tokens": mate})
        grad = mm_tn(kv[2 * b].reshape(count, DH), dgu[...].reshape(count, DH)).astype(BF16)
        gg_s[b, GATE] = grad[:, :half]
        send(gg_s.at[b, GATE], gg_r.at[b, GATE], x_s.at[b], x_r.at[b, GATE], {"tokens": mate})
        gg_s[b, UP] = grad[:, half:]
        send(gg_s.at[b, UP], gg_r.at[b, UP], x_s.at[b], x_r.at[b, UP], {"tokens": mate})

    def exchange(b, m):
        if m == DOWN:
            mine, theirs, full = gd_s.at[b], gd_r.at[b], full_d
        else:
            mine, theirs, full = gg_s.at[b, m], gg_r.at[b, m], full_g.at[m]
        arrived(theirs, x_r.at[b, m])
        total = (mine[...].astype(F32) + theirs[...].astype(F32)).astype(BF16)
        full[b, core] = total
        here = full.at[b, core]
        if b == 0:
            send(here, here, c_s.at[b], c_r.at[b, m], twin)
        else:
            @pl.when(away)
            def _():
                send(here, here, c_s.at[b], c_r.at[b, m], twin)

    def whole(b, m):
        full = full_d if m == DOWN else full_g.at[m]
        arrived(full.at[b, 1 - core], c_r.at[b, m])
        if m == DOWN:
            return full_d[b].reshape(DH, DH)
        return jnp.concatenate([full_g[m, b, 0], full_g[m, b, 1]], axis=1)

    @pl.when(home)
    def _():
        own_w.wait()

    @pl.when(away)
    def _():
        arrived(w_own, w_sem.at[0])

    halve_weights(w_own)
    gradients(0, w_own)
    if EARLY < 1:
        spread_keys(1)
    if EARLY < 2:
        spread_values(1)
    local_gain.wait()
    finish_block(0, lambda h: y0[:, h * DH:(h + 1) * DH])
    for m in ORDER:
        exchange(0, m)
    if EARLY < 3:
        spread_queries()

    @pl.when(away)
    def _():
        for array in (2, 3):
            for k in range(8):
                i = slot(k)
                arrived(kv.at[array, i], kv_r.at[array, i])
                send(kv.at[array, i], kv.at[array, i], fwd_s.at[array], kv_r.at[array, i], twin)

    updates = orthogonalize([whole(0, m) for m in ORDER])
    for m, update in zip(ORDER, updates):
        w1[m] = (w_own[m].astype(F32) + step_size * update.astype(F32)).astype(BF16)
    halve_weights(w1)
    gradients(1, w1)

    @pl.when(away)
    def _():
        for k in range(8):
            i = slot(k)
            arrived(qb.at[i], q_r.at[i])
            if k >= 4:
                send(qb.at[i], qb.at[i], fwd_s.at[4], q_r.at[i], twin)

    for k in range(4):
        i = slot(k, home_bit)

        @pl.when(home)
        def _():
            arrived(qb.at[i], q_r.at[i])

        ysend[k] = fast_net(qb[i], w1[GATE], w1[UP], w1[DOWN]).astype(BF16)
        send(ysend.at[k], ybuf.at[own_head], y_sem.at[0], y_sem.at[1],
             {"heads": kind, "tokens": group_tokens(k, home_bit)})

    for m in ORDER:
        exchange(1, m)

    def squares_of_block1():
        arrived(ybuf, y_sem.at[1])
        square = jnp.zeros((rows, 1), F32)
        for h in range(HL):
            out = ybuf[h].astype(F32)
            square = square + jnp.sum(out * out, axis=1, keepdims=True)
        share_squares(1, square)

    def pass_c(m, j, device):
        part = wout.at[j, m]
        send(part, part, dist_s.at[0], dc_r.at[j, m], {"tokens": device})

    def rows_of(j, m, which):
        return wout.at[j, m, pl.ds(pl.multiple_of(which * half, half), half)]

    def pass_s(m, j, which, device):
        part = rows_of(j, m, which)
        send(part, part, dist_s.at[0], ds_r.at[j, m, which], {"tokens": device})

    def along_z(m, j, up, down):
        @pl.when((z < 3) & up)
        def _():
            pass_s(m, j, y, t + 4)

        @pl.when((z > 0) & down)
        def _():
            pass_s(m, j, y, t - 4)

    def start_spread(m):
        @pl.when(core == 0)
        def _():
            pass_c(m, own_head, y_near)
            pass_c(m, own_head, z_near)
            pass_c(m, own_head, x_near)

        @pl.when(core == 1)
        def _():
            pass_s(m, own_head, 1 - y, y_near)
            along_z(m, own_head, True, True)
            pass_s(m, own_head, y, y_near)

    @pl.when(home)
    def _():
        for m in ORDER:
            (update,) = orthogonalize([whole(1, m)])
            wout[own_head, m] = (w1[m].astype(F32) + step_size * update.astype(F32)).astype(BF16)
            start_spread(m)
            if m == ORDER[0]:
                squares_of_block1()

    @pl.when(away)
    def _():
        squares_of_block1()

    @pl.when(core == 0)
    def _():
        near, far = x + 2 * zl, x + 2 * (1 - zl)
        for m in ORDER:
            @pl.when(kind == 1)
            def _():
                arrived(wout.at[near, m], dc_r.at[near, m])
                pass_c(m, near, z_near)
                pass_c(m, near, x_near)

            arrived(wout.at[far, m], dc_r.at[far, m])
            pass_c(m, far, x_near)

    @pl.when(core == 1)
    def _():
        def first(m):
            @pl.when(kind == 0)
            def _():
                arrived(rows_of(z, m, y), ds_r.at[z, m, y])
                along_z(m, z, True, True)

        def later(m, d):
            @pl.when(z >= d)
            def _():
                arrived(rows_of(z - d, m, y), ds_r.at[z - d, m, y])
                along_z(m, z - d, True, False)
                pass_s(m, z - d, y, y_near)

            @pl.when(z + d <= 3)
            def _():
                arrived(rows_of(z + d, m, y), ds_r.at[z + d, m, y])
                along_z(m, z + d, False, True)
                pass_s(m, z + d, y, y_near)

        for step in range(6):
            for i, m in enumerate(ORDER):
                d = step - i
                if d == 0:
                    first(m)
                elif 1 <= d <= 3:
                    later(m, d)

    finish_block(1, lambda h: ybuf[h].astype(F32))

    @pl.when(core == 0)
    def _():
        for m in ORDER:
            for j in (1 - x + 2 * zl, 1 - x + 2 * (1 - zl)):
                arrived(wout.at[j, m], dc_r.at[j, m])
        drained(wout.at[pl.ds(0, 3)], dist_s.at[0])

        @pl.when(kind == 0)
        def _():
            drained(wout.at[0], dist_s.at[0])

    @pl.when(core == 1)
    def _():
        for m in ORDER:
            for d in range(4):
                j = (z + d) % 4
                if d == 0:
                    @pl.when(kind == 0)
                    def _():
                        arrived(rows_of(j, m, 1 - y), ds_r.at[j, m, 1 - y])
                else:
                    arrived(rows_of(j, m, 1 - y), ds_r.at[j, m, 1 - y])
        drained(wout.at[0, :, pl.ds(0, half)], dist_s.at[0])
        drained(wout.at[0], dist_s.at[0])

        @pl.when(kind == 1)
        def _():
            drained(wout.at[0], dist_s.at[0])

        drained(wout.at[0, :, pl.ds(0, half)], dist_s.at[0])

        @pl.when((z == 1) | (z == 2))
        def _():
            drained(wout.at[pl.ds(0, 2)], dist_s.at[0])

    for i in range(5):
        drained(qb.at[pl.ds(0, HL)], a2a_s.at[i])

    @pl.when(away)
    def _():
        for i in range(4):
            drained(qb, fwd_s.at[i])
        drained(qb.at[pl.ds(0, 4)], fwd_s.at[4])
        drained(full_d.at[0], c_s.at[1])
        drained(full_d.at[0, 0], c_s.at[1])

    @pl.when(home)
    def _():
        drained(w_own, fwd_s.at[5])

    for b in range(2):
        drained(full_d.at[0], x_s.at[b])
        drained(full_d.at[0, 0], x_s.at[b])
        drained(sqr.at[b], sq_s.at[b])
    drained(full_d.at[0], c_s.at[0])
    drained(full_d.at[0, 0], c_s.at[0])
    drained(ysend, y_sem.at[0])


SPREAD = (2, 1, 3, 0)
EARLY = 2


def one_kernel(cores, queries, keys, values, rates, fast_init, out_gain):
    blocks, rows, width = queries.shape
    HL, _, DH, _ = fast_init.shape
    half = DH // 2
    dma = lambda *shape: pltpu.SemaphoreType.DMA(shape)
    vm = pltpu.VMEM
    any_space = pl.BlockSpec(memory_space=pl.ANY)
    in_vmem = pl.BlockSpec(memory_space=pltpu.VMEM)
    return pl.pallas_call(
        functools.partial(kernel, (cores, HL, rows, DH)),
        out_shape=(pltpu.VMEM(queries.shape, BF16), pltpu.VMEM(fast_init.shape, BF16)),
        in_specs=[any_space] * 6,
        out_specs=(in_vmem, in_vmem),
        scratch_shapes=[
            vm((rows, width), BF16),
            vm((2, rows, width), BF16),
            vm(fast_init.shape, BF16),
            vm(rates.shape, F32),
            vm((1, width), F32),
            vm((2, HL, rows, DH), BF16),
            vm((4, 8, rows, DH), BF16),
            vm((8, rows, DH), BF16),
            vm((8, rows, DH), F32),
            vm((8, rows, DH), BF16),
            vm((8, rows, half), BF16),
            vm((3, DH, DH), BF16),
            vm((3, DH, DH), BF16),
            vm((2, DH, DH), BF16),
            vm((2, half, DH), BF16),
            vm((2, half, DH), BF16),
            vm((2, 2, DH, half), BF16),
            vm((2, 2, DH, half), BF16),
            vm((2, 2, half, DH), BF16),
            vm((2, 2, 2, DH, half), BF16),
            vm((HL, rows, DH), BF16),
            vm((HL, rows, DH), BF16),
            vm((rows, width), F32),
            vm((2, rows, 128), F32),
            vm((2, rows, 128), F32),
            dma(6),
            dma(5), dma(4, 8), dma(8), dma(1), dma(6),
            dma(2), dma(2, 3), dma(2), dma(2, 3),
            dma(2), dma(2), dma(2),
            dma(4, 3), dma(4, 3, 2), dma(1),
        ],
        compiler_params=pltpu.CompilerParams(collective_id=0, has_side_effects=True),
    )(queries, keys, values, rates, fast_init, out_gain.reshape(1, width))


def fits(cores, token_devices, queries, fast_init):
    blocks, rows, width = queries.shape
    HL, _, DH, _ = fast_init.shape
    return (
        blocks == 2 and HL == 4 and cores == 2 and token_devices == 16
        and rows == 128 and DH == 256
    )


def per_device_best(cores, token_devices, queries, keys, values, rates, fast_init, out_gain):
    if fits(cores, token_devices, queries, fast_init):
        return one_kernel(cores, queries, keys, values, rates, fast_init, out_gain)
    return per_device(queries, keys, values, rates, fast_init, out_gain)


def solution(mesh):
    in_specs = (
        P(None, "tokens", "heads"),
        P(None, "tokens", "heads"),
        P(None, "tokens", "heads"),
        P(None, "heads", "tokens"),
        P("heads", None, None, None),
        P("heads"),
    )
    out_specs = (P(None, "tokens", "heads"), P("heads", None, None, None))
    return jax.shard_map(
        functools.partial(per_device_best, mesh.shape["heads"], mesh.shape["tokens"]), mesh=mesh, in_specs=in_specs, out_specs=out_specs, check_vma=False
    )
```

```python
import functools

import jax
import jax.numpy as jnp
from jax import lax
from jax.experimental import pallas as pl
from jax.experimental.pallas import tpu as pltpu
from jax.sharding import PartitionSpec as P

D = 2048
NS_STEPS = 2


coef_a = 3.4445
coef_b = -4.775
coef_c = 2.0315
step_size = 0.5


def newton(current):
    for step in range(NS_STEPS):
        gram = jnp.einsum(
            "hmij,hmkj->hmik", current, current, preferred_element_type=jnp.float32
        ).astype(jnp.bfloat16)
        square = jnp.einsum("hmij,hmjk->hmik", gram, gram, preferred_element_type=jnp.float32)
        mixer = (coef_b * gram.astype(jnp.float32) + coef_c * square).astype(jnp.bfloat16)
        product = jnp.einsum("hmij,hmjk->hmik", mixer, current, preferred_element_type=jnp.float32)
        current = (coef_a * current.astype(jnp.float32) + product).astype(jnp.bfloat16)
    return current


def apply_heads(query, weights):
    gate_q = jnp.einsum("nhd,hde->nhe", query, weights[:, 0], preferred_element_type=jnp.float32)
    up_q = jnp.einsum("nhd,hde->nhe", query, weights[:, 1], preferred_element_type=jnp.float32)
    hidden_q = (jax.nn.silu(gate_q) * up_q).astype(jnp.bfloat16)
    return jnp.einsum("nhd,hde->nhe", hidden_q, weights[:, 2], preferred_element_type=jnp.float32)


def local_grads(key_rows, value_rows, rate, weights):
    gate_k = jnp.einsum("nhd,hde->nhe", key_rows, weights[:, 0], preferred_element_type=jnp.float32)
    up_k = jnp.einsum("nhd,hde->nhe", key_rows, weights[:, 1], preferred_element_type=jnp.float32)
    sig = jax.nn.sigmoid(gate_k)
    hidden = (gate_k * sig * up_k).astype(jnp.bfloat16)
    scaled = (rate.T[:, :, None] * value_rows.astype(jnp.float32)).astype(jnp.bfloat16)
    back = jnp.einsum("nhe,hde->nhd", scaled, weights[:, 2], preferred_element_type=jnp.float32)
    grad_gate = (back * up_k * sig * (1.0 + gate_k * (1.0 - sig))).astype(jnp.bfloat16)
    grad_up = (back * gate_k * sig).astype(jnp.bfloat16)
    g_gate = jnp.einsum("nhd,nhe->hde", key_rows, grad_gate, preferred_element_type=jnp.float32)
    g_up = jnp.einsum("nhd,nhe->hde", key_rows, grad_up, preferred_element_type=jnp.float32)
    g_down = jnp.einsum("nhd,nhe->hde", hidden, scaled, preferred_element_type=jnp.float32)
    return jnp.stack([g_gate, g_up, g_down], axis=1)


def finish(joined, totals, out_gain):
    return (joined / jnp.sqrt(totals[:, None] / D + 1e-06) * out_gain[None, :]).astype(jnp.bfloat16)


def per_device(queries, keys, values, rates, fast_init, out_gain):
    heads_here = fast_init.shape[0]
    head_size = fast_init.shape[2]
    tok_rows = queries.shape[1]
    weights = fast_init
    outputs = []
    joined_all = []
    for block in range(queries.shape[0]):
        query = queries[block].reshape(tok_rows, heads_here, head_size)
        key_rows = keys[block].reshape(tok_rows, heads_here, head_size)
        value_rows = values[block].reshape(tok_rows, heads_here, head_size)
        joined = apply_heads(query, weights).reshape(tok_rows, heads_here * head_size)
        grads = local_grads(key_rows, value_rows, rates[block], weights)
        total = lax.psum(grads, "tokens")
        squares = jnp.sum(total * total, axis=(2, 3))
        start = (total / (jnp.sqrt(squares)[:, :, None, None] + 1e-07)).astype(jnp.bfloat16)
        update = newton(start)
        weights = (weights.astype(jnp.float32) + step_size * update.astype(jnp.float32)).astype(
            jnp.bfloat16
        )
        joined_all.append(joined)
    stacked = jnp.stack(joined_all, axis=0)
    totals = lax.psum(jnp.sum(stacked * stacked, axis=2), "heads")
    outputs = [
        finish(joined_all[index], totals[index], out_gain) for index in range(len(joined_all))
    ]
    return (jnp.stack(outputs, axis=0), weights)


F32 = jnp.float32
BF16 = jnp.bfloat16
MESH = pl.DeviceIdType.MESH
DOWN, GATE, UP = 2, 0, 1
ORDER = (DOWN, GATE, UP)


def mm(a, b):
    return jnp.dot(a, b, preferred_element_type=F32)


def mm_nt(a, b):
    return lax.dot_general(a, b, (((1,), (1,)), ((), ())), preferred_element_type=F32)


def mm_tn(a, b):
    return lax.dot_general(a, b, (((0,), (0,)), ((), ())), preferred_element_type=F32)


def orthogonalize(mats):
    xs = []
    for g in mats:
        g = g.astype(F32)
        square = jnp.sum(jnp.sum(g * g, axis=1, keepdims=True), axis=0, keepdims=True)
        xs.append((g / (jnp.sqrt(square) + 1e-07)).astype(BF16))
    for _ in range(NS_STEPS):
        grams = [mm_nt(x, x).astype(BF16) for x in xs]
        mixers = [(coef_b * a.astype(F32) + coef_c * mm(a, a)).astype(BF16) for a in grams]
        xs = [(coef_a * x.astype(F32) + mm(b, x)).astype(BF16) for b, x in zip(mixers, xs)]
    return xs


def kernel(
    sizes, q_hbm, k_hbm, v_hbm, r_hbm, w_hbm, gain_hbm, mixed, wout,
    q0, vals, w0, rates, gain, dps, kv, qb, act, dgu, hid, w_own, w1, wgu, gd_s, gd_r, gg_s, gg_r, full_d, full_g,
    ysend, ybuf, y0, sq, sqr,
    loc_sem, a2a_s, kv_r, q_r, w_sem, fwd_s, x_s, x_r, c_s, c_r, y_sem, sq_s, sq_r, dist_r, dist_s,
):
    cores, HL, rows, DH = sizes
    width = HL * DH
    half = DH // 2
    core = lax.axis_index("heads")
    t = lax.axis_index("tokens")
    x, y, zl, zh = t % 2, (t // 2) % 2, (t // 4) % 2, t // 8
    z = t // 4
    kind = (x + y + zl) % 2
    home = core == kind
    away = core != kind

    own_slot = x + 2 * y + 4 * zl
    own_head = x + 2 * zl
    mate = t + 8 * (1 - 2 * zh)
    x_near = t + 1 - 2 * x
    y_near = t + 2 * (1 - 2 * y)
    z_near = t + 4 * (1 - 2 * zl)

    def slot(k):
        return (x + k % 2) % 2 + 2 * ((y + k // 2 % 2) % 2) + 4 * ((zl + k // 4) % 2)

    def head_at(dx, dz):
        return (x + dx) % 2 + 2 * ((zl + dz) % 2)

    def owner(dx, dz):
        x0, z0 = (x + dx) % 2, (zl + dz) % 2
        return x0 + 2 * ((x0 + z0 + core) % 2) + 4 * z0 + 8 * zh

    def remote(src, dst, send_sem, recv_sem, device):
        return pltpu.make_async_remote_copy(
            src_ref=src, dst_ref=dst, send_sem=send_sem, recv_sem=recv_sem,
            device_id=device, device_id_type=MESH,
        )

    def send(src, dst, send_sem, recv_sem, device):
        remote(src, dst, send_sem, recv_sem, device).start()

    def arrived(ref, recv_sem):
        remote(ref, ref, loc_sem.at[0], recv_sem, {"tokens": x_near}).wait_recv()

    def drained(ref, send_sem):
        remote(ref, ref, send_sem, loc_sem.at[0], {"tokens": x_near}).wait_send()

    def cols(h):
        return pl.ds(pl.multiple_of(h * DH, DH), DH)

    twin = {"heads": 1 - core}

    local_v = [pltpu.make_async_copy(v_hbm.at[b], vals.at[b], loc_sem.at[4 + b]) for b in range(2)]
    local_r = pltpu.make_async_copy(r_hbm, rates, loc_sem.at[2])
    local_q = pltpu.make_async_copy(q_hbm.at[0], q0, loc_sem.at[0])
    local_w = pltpu.make_async_copy(w_hbm, w0, loc_sem.at[1])
    local_gain = pltpu.make_async_copy(gain_hbm, gain, loc_sem.at[3])
    own_w = pltpu.make_async_copy(w_hbm.at[own_head], w_own, w_sem.at[0])
    local_r.start()
    local_v[0].start()
    local_w.start()
    local_q.start()
    local_v[1].start()
    local_gain.start()

    @pl.when(home)
    def _():
        own_w.start()

    barrier = pltpu.get_barrier_semaphore()

    @pl.when(away)
    def _():
        for k in range(8):
            pl.semaphore_signal(
                barrier, inc=1, device_id={"heads": 1 - core, "tokens": slot(k) + 8 * zh}, device_id_type=MESH
            )

    for device in ({"heads": 1 - core}, *({"tokens": chip} for chip in (mate, x_near, y_near, z_near))):
        pl.semaphore_signal(barrier, inc=1, device_id=device, device_id_type=MESH)
    pl.semaphore_wait(barrier, HL + 5)

    def spread(array, view, landing, recv_sems):
        for dx, dz in SPREAD:
            send(view(head_at(dx, dz)), landing.at[own_slot], a2a_s.at[array], recv_sems.at[own_slot],
                 {"heads": 1 - core, "tokens": owner(dx, dz)})

    def spread_keys(b):
        spread(2 * b, lambda j: k_hbm.at[b, :, cols(j)], kv.at[2 * b], kv_r.at[2 * b])

    def spread_values(b):
        spread(2 * b + 1, lambda j: dps.at[b, j], kv.at[2 * b + 1], kv_r.at[2 * b + 1])

    def spread_queries():
        spread(4, lambda j: q_hbm.at[1, :, cols(j)], qb, q_r)

    def scale_values(b):
        for j in range(HL):
            rate = jnp.broadcast_to(rates[b, pl.ds(j, 1), :], (rows, rows)).T[:, :1]
            dps[b, j] = (rate * vals[b, :, j * DH:(j + 1) * DH].astype(F32)).astype(BF16)

    def issue(point):
        for when, what in zip(ISSUE, (lambda: spread_keys(1), lambda: spread_values(1), spread_queries)):
            if when == point:
                what()

    spread_keys(0)

    @pl.when(home)
    def _():
        send(w_hbm.at[own_head], w_own, fwd_s.at[5], w_sem.at[0], twin)

    local_r.wait()
    local_v[0].wait()
    scale_values(0)
    spread_values(0)
    local_v[1].wait()
    scale_values(1)
    issue(0)

    def share_squares(b, square):
        sq[b] = jnp.broadcast_to(square, (rows, 128))
        send(sq.at[b], sqr.at[b], sq_s.at[b], sq_r.at[b], twin)

    def finish_block(b, read):
        total = sq[b]
        arrived(sqr.at[b], sq_r.at[b])
        total = total + sqr[b]
        root = jnp.sqrt(total[:, :1] / (cores * width) + 1e-06)
        for h in range(HL):
            span = slice(h * DH, (h + 1) * DH)
            mixed[b, :, span] = (read(h) / root * gain[:, span]).astype(BF16)

    def fast_net(rows_in, w_gate, w_up, w_down):
        gate = mm(rows_in, w_gate)
        hidden = (jax.nn.silu(gate) * mm(rows_in, w_up)).astype(BF16)
        return mm(hidden, w_down)

    local_w.wait()
    local_q.wait()
    square = jnp.zeros((rows, 1), F32)
    for h in range(HL):
        span = slice(h * DH, (h + 1) * DH)
        out = fast_net(q0[:, span], w0[h, 0], w0[h, 1], w0[h, 2])
        y0[:, span] = out
        square = square + jnp.sum(out * out, axis=1, keepdims=True)
    share_squares(0, square)

    def halve_weights(w):
        for c in range(2):
            span = slice(c * half, (c + 1) * half)
            wgu[c] = jnp.concatenate([w[GATE, :, span], w[UP, :, span]], axis=1)

    def forward(array, i, when):
        @pl.when(when)
        def _():
            send(kv.at[array, i], kv.at[array, i], fwd_s.at[array], kv_r.at[array, i], twin)

    def gradients(b, w):
        weights = wgu[core]
        w_down = w[DOWN, pl.ds(pl.multiple_of(core * half, half), half), :]
        def activations(i, gate_up, back):
            gate = gate_up[:, :half]
            up = gate_up[:, half:]
            sig = jax.nn.sigmoid(gate)
            hid[i] = (gate * sig * up).astype(BF16)
            dgu[i, :, :half] = (back * up * sig * (1.0 + gate * (1.0 - sig))).astype(BF16)
            dgu[i, :, half:] = (back * gate * sig).astype(BF16)

        if b == 0:
            for k in range(8):
                i = slot(k)
                arrived(kv.at[0, i], kv_r.at[0, i])
                forward(0, i, away)
                act[k] = mm(kv[0, i], weights)
            for k in range(8):
                i = slot(k)
                arrived(kv.at[1, i], kv_r.at[1, i])
                forward(1, i, away)
                activations(i, act[k], mm_nt(kv[1, i], w_down))
                if k == 3:
                    issue(1)
            issue(2)
        else:
            @pl.when(home)
            def _():
                for k in range(8):
                    i = slot(k)
                    arrived(kv.at[2, i], kv_r.at[2, i])
                    arrived(kv.at[3, i], kv_r.at[3, i])

            for i in range(8):
                activations(i, mm(kv[2, i], weights), mm_nt(kv[3, i], w_down))
        count = 8 * rows
        grad = mm_tn(hid[...].reshape(count, half), kv[2 * b + 1].reshape(count, DH))
        gd_s[b] = grad.astype(BF16)
        send(gd_s.at[b], gd_r.at[b], x_s.at[b], x_r.at[b, DOWN], {"tokens": mate})
        grad = mm_tn(kv[2 * b].reshape(count, DH), dgu[...].reshape(count, DH)).astype(BF16)
        gg_s[b, GATE] = grad[:, :half]
        send(gg_s.at[b, GATE], gg_r.at[b, GATE], x_s.at[b], x_r.at[b, GATE], {"tokens": mate})
        gg_s[b, UP] = grad[:, half:]
        send(gg_s.at[b, UP], gg_r.at[b, UP], x_s.at[b], x_r.at[b, UP], {"tokens": mate})

    def exchange(b, m):
        if m == DOWN:
            mine, theirs, full = gd_s.at[b], gd_r.at[b], full_d
        else:
            mine, theirs, full = gg_s.at[b, m], gg_r.at[b, m], full_g.at[m]
        arrived(theirs, x_r.at[b, m])
        total = (mine[...].astype(F32) + theirs[...].astype(F32)).astype(BF16)
        full[b, core] = total
        here = full.at[b, core]
        if b == 0:
            send(here, here, c_s.at[b], c_r.at[b, m], twin)
        else:
            @pl.when(away)
            def _():
                send(here, here, c_s.at[b], c_r.at[b, m], twin)

    def whole(b, m):
        full = full_d if m == DOWN else full_g.at[m]
        arrived(full.at[b, 1 - core], c_r.at[b, m])
        if m == DOWN:
            return full_d[b].reshape(DH, DH)
        return jnp.concatenate([full_g[m, b, 0], full_g[m, b, 1]], axis=1)

    @pl.when(home)
    def _():
        own_w.wait()

    @pl.when(away)
    def _():
        arrived(w_own, w_sem.at[0])

    halve_weights(w_own)
    gradients(0, w_own)
    issue(3)
    local_gain.wait()
    finish_block(0, lambda h: y0[:, h * DH:(h + 1) * DH])
    for m in ORDER:
        exchange(0, m)
    issue(4)

    def pass_on(array):
        @pl.when(away)
        def _():
            for k in range(8):
                i = slot(k)
                arrived(kv.at[array, i], kv_r.at[array, i])
                send(kv.at[array, i], kv.at[array, i], fwd_s.at[array], kv_r.at[array, i], twin)

    if PASS_EARLY >= 1:
        pass_on(2)
    if PASS_EARLY >= 2:
        pass_on(3)
    updates = orthogonalize([whole(0, m) for m in ORDER])
    if PASS_EARLY < 1:
        pass_on(2)
    if PASS_EARLY < 2:
        pass_on(3)
    for m, update in zip(ORDER, updates):
        w1[m] = (w_own[m].astype(F32) + step_size * update.astype(F32)).astype(BF16)
    halve_weights(w1)
    gradients(1, w1)

    @pl.when(away)
    def _():
        for i in range(8):
            arrived(qb.at[i], q_r.at[i])
        for i in range(8):
            ysend[i] = fast_net(qb[i], w1[GATE], w1[UP], w1[DOWN]).astype(BF16)
            send(ysend.at[i], ybuf.at[own_head], y_sem.at[0], y_sem.at[1], {"heads": kind, "tokens": i + 8 * zh})

    for m in ORDER:
        exchange(1, m)

    def squares_of_block1():
        arrived(ybuf, y_sem.at[1])
        square = jnp.zeros((rows, 1), F32)
        for h in range(HL):
            out = ybuf[h].astype(F32)
            square = square + jnp.sum(out * out, axis=1, keepdims=True)
        share_squares(1, square)

    def rows_of(j, m, which):
        return wout.at[j, m, pl.ds(which * half, half)]

    def wait_part(j, m, which):
        arrived(rows_of(j, m, which), dist_r.at[j, m, which])

    def pass_part(j, m, which, device):
        part = rows_of(j, m, which)
        send(part, part, dist_s.at[0], dist_r.at[j, m, which], {"tokens": device})

    def start_spread(m):
        for which in range(2):
            for chip in (x_near, y_near, z_near):
                pass_part(own_head, m, which, chip)

    @pl.when(home)
    def _():
        for m in ORDER:
            (update,) = orthogonalize([whole(1, m)])
            wout[own_head, m] = (w1[m].astype(F32) + step_size * update.astype(F32)).astype(BF16)
            start_spread(m)

    by_x, by_y, by_z = head_at(1, 0), head_at(0, 0), head_at(0, 1)
    opposite = head_at(1, 1)

    @pl.when(away)
    def _():
        for m in ORDER:
            if m == ORDER[2]:
                squares_of_block1()
            for which in range(2):
                for j, chip in ((by_x, z_near), (by_y, x_near), (by_z, y_near)):
                    wait_part(j, m, which)
                    pass_part(j, m, which, chip)

    relays = ((by_z, x_near), (opposite, y_near), (by_x, z_near))

    @pl.when(home)
    def _():
        for n, (m, (j, chip)) in enumerate(zip(ORDER, relays)):
            if n == 2:
                squares_of_block1()
            for which in range(2):
                wait_part(j, m, which)
                pass_part(j, m, which, chip)

    finish_block(1, lambda h: ybuf[h].astype(F32))

    @pl.when(away)
    def _():
        for m in ORDER:
            for which in range(2):
                wait_part(opposite, m, which)

    @pl.when(home)
    def _():
        for m, (relayed, _) in zip(ORDER, relays):
            for j, _ in relays:
                if j is not relayed:
                    for which in range(2):
                        wait_part(j, m, which)

    drained(wout.at[pl.ds(0, 3)], dist_s.at[0])

    @pl.when(home)
    def _():
        drained(wout.at[0], dist_s.at[0])

    for i in range(5):
        drained(qb.at[pl.ds(0, HL)], a2a_s.at[i])

    @pl.when(away)
    def _():
        for i in range(4):
            drained(qb, fwd_s.at[i])
        drained(ysend, y_sem.at[0])
        drained(full_d.at[0], c_s.at[1])
        drained(full_d.at[0, 0], c_s.at[1])

    @pl.when(home)
    def _():
        drained(w_own, fwd_s.at[5])

    for b in range(2):
        drained(full_d.at[0], x_s.at[b])
        drained(full_d.at[0, 0], x_s.at[b])
        drained(sqr.at[b], sq_s.at[b])
    drained(full_d.at[0], c_s.at[0])
    drained(full_d.at[0, 0], c_s.at[0])


SPREAD = ((1, 1), (1, 0), (0, 1), (0, 0))
ISSUE = (0, 1, 4)
PASS_EARLY = 2


def one_kernel(cores, queries, keys, values, rates, fast_init, out_gain):
    blocks, rows, width = queries.shape
    HL, _, DH, _ = fast_init.shape
    half = DH // 2
    dma = lambda *shape: pltpu.SemaphoreType.DMA(shape)
    vm = pltpu.VMEM
    any_space = pl.BlockSpec(memory_space=pl.ANY)
    in_vmem = pl.BlockSpec(memory_space=pltpu.VMEM)
    return pl.pallas_call(
        functools.partial(kernel, (cores, HL, rows, DH)),
        out_shape=(pltpu.VMEM(queries.shape, BF16), pltpu.VMEM(fast_init.shape, BF16)),
        in_specs=[any_space] * 6,
        out_specs=(in_vmem, in_vmem),
        scratch_shapes=[
            vm((rows, width), BF16),
            vm((2, rows, width), BF16),
            vm(fast_init.shape, BF16),
            vm(rates.shape, F32),
            vm((1, width), F32),
            vm((2, HL, rows, DH), BF16),
            vm((4, 8, rows, DH), BF16),
            vm((8, rows, DH), BF16),
            vm((8, rows, DH), F32),
            vm((8, rows, DH), BF16),
            vm((8, rows, half), BF16),
            vm((3, DH, DH), BF16),
            vm((3, DH, DH), BF16),
            vm((2, DH, DH), BF16),
            vm((2, half, DH), BF16),
            vm((2, half, DH), BF16),
            vm((2, 2, DH, half), BF16),
            vm((2, 2, DH, half), BF16),
            vm((2, 2, half, DH), BF16),
            vm((2, 2, 2, DH, half), BF16),
            vm((8, rows, DH), BF16),
            vm((HL, rows, DH), BF16),
            vm((rows, width), F32),
            vm((2, rows, 128), F32),
            vm((2, rows, 128), F32),
            dma(6),
            dma(5), dma(4, 8), dma(8), dma(1), dma(6),
            dma(2), dma(2, 3), dma(2), dma(2, 3),
            dma(2), dma(2), dma(2),
            dma(4, 3, 2), dma(1),
        ],
        compiler_params=pltpu.CompilerParams(collective_id=0, has_side_effects=True),
    )(queries, keys, values, rates, fast_init, out_gain.reshape(1, width))


def fits(cores, token_devices, queries, fast_init):
    blocks, rows, width = queries.shape
    HL, _, DH, _ = fast_init.shape
    return (
        blocks == 2 and HL == 4 and cores == 2 and token_devices == 16
        and rows == 128 and DH == 256
    )


def per_device_best(cores, token_devices, queries, keys, values, rates, fast_init, out_gain):
    if fits(cores, token_devices, queries, fast_init):
        return one_kernel(cores, queries, keys, values, rates, fast_init, out_gain)
    return per_device(queries, keys, values, rates, fast_init, out_gain)


def solution(mesh):
    in_specs = (
        P(None, "tokens", "heads"),
        P(None, "tokens", "heads"),
        P(None, "tokens", "heads"),
        P(None, "heads", "tokens"),
        P("heads", None, None, None),
        P("heads"),
    )
    out_specs = (P(None, "tokens", "heads"), P("heads", None, None, None))
    return jax.shard_map(
        functools.partial(per_device_best, mesh.shape["heads"], mesh.shape["tokens"]), mesh=mesh, in_specs=in_specs, out_specs=out_specs, check_vma=False
    )
```

```python
import functools

import jax
import jax.numpy as jnp
from jax import lax
from jax.experimental import pallas as pl
from jax.experimental.pallas import tpu as pltpu
from jax.sharding import PartitionSpec as P

D = 2048
NS_STEPS = 2


coef_a = 3.4445
coef_b = -4.775
coef_c = 2.0315
step_size = 0.5


def newton(current):
    for step in range(NS_STEPS):
        gram = jnp.einsum(
            "hmij,hmkj->hmik", current, current, preferred_element_type=jnp.float32
        ).astype(jnp.bfloat16)
        square = jnp.einsum("hmij,hmjk->hmik", gram, gram, preferred_element_type=jnp.float32)
        mixer = (coef_b * gram.astype(jnp.float32) + coef_c * square).astype(jnp.bfloat16)
        product = jnp.einsum("hmij,hmjk->hmik", mixer, current, preferred_element_type=jnp.float32)
        current = (coef_a * current.astype(jnp.float32) + product).astype(jnp.bfloat16)
    return current


def apply_heads(query, weights):
    gate_q = jnp.einsum("nhd,hde->nhe", query, weights[:, 0], preferred_element_type=jnp.float32)
    up_q = jnp.einsum("nhd,hde->nhe", query, weights[:, 1], preferred_element_type=jnp.float32)
    hidden_q = (jax.nn.silu(gate_q) * up_q).astype(jnp.bfloat16)
    return jnp.einsum("nhd,hde->nhe", hidden_q, weights[:, 2], preferred_element_type=jnp.float32)


def local_grads(key_rows, value_rows, rate, weights):
    gate_k = jnp.einsum("nhd,hde->nhe", key_rows, weights[:, 0], preferred_element_type=jnp.float32)
    up_k = jnp.einsum("nhd,hde->nhe", key_rows, weights[:, 1], preferred_element_type=jnp.float32)
    sig = jax.nn.sigmoid(gate_k)
    hidden = (gate_k * sig * up_k).astype(jnp.bfloat16)
    scaled = (rate.T[:, :, None] * value_rows.astype(jnp.float32)).astype(jnp.bfloat16)
    back = jnp.einsum("nhe,hde->nhd", scaled, weights[:, 2], preferred_element_type=jnp.float32)
    grad_gate = (back * up_k * sig * (1.0 + gate_k * (1.0 - sig))).astype(jnp.bfloat16)
    grad_up = (back * gate_k * sig).astype(jnp.bfloat16)
    g_gate = jnp.einsum("nhd,nhe->hde", key_rows, grad_gate, preferred_element_type=jnp.float32)
    g_up = jnp.einsum("nhd,nhe->hde", key_rows, grad_up, preferred_element_type=jnp.float32)
    g_down = jnp.einsum("nhd,nhe->hde", hidden, scaled, preferred_element_type=jnp.float32)
    return jnp.stack([g_gate, g_up, g_down], axis=1)


def finish(joined, totals, out_gain):
    return (joined / jnp.sqrt(totals[:, None] / D + 1e-06) * out_gain[None, :]).astype(jnp.bfloat16)


def per_device(queries, keys, values, rates, fast_init, out_gain):
    heads_here = fast_init.shape[0]
    head_size = fast_init.shape[2]
    tok_rows = queries.shape[1]
    weights = fast_init
    outputs = []
    joined_all = []
    for block in range(queries.shape[0]):
        query = queries[block].reshape(tok_rows, heads_here, head_size)
        key_rows = keys[block].reshape(tok_rows, heads_here, head_size)
        value_rows = values[block].reshape(tok_rows, heads_here, head_size)
        joined = apply_heads(query, weights).reshape(tok_rows, heads_here * head_size)
        grads = local_grads(key_rows, value_rows, rates[block], weights)
        total = lax.psum(grads, "tokens")
        squares = jnp.sum(total * total, axis=(2, 3))
        start = (total / (jnp.sqrt(squares)[:, :, None, None] + 1e-07)).astype(jnp.bfloat16)
        update = newton(start)
        weights = (weights.astype(jnp.float32) + step_size * update.astype(jnp.float32)).astype(
            jnp.bfloat16
        )
        joined_all.append(joined)
    stacked = jnp.stack(joined_all, axis=0)
    totals = lax.psum(jnp.sum(stacked * stacked, axis=2), "heads")
    outputs = [
        finish(joined_all[index], totals[index], out_gain) for index in range(len(joined_all))
    ]
    return (jnp.stack(outputs, axis=0), weights)


F32 = jnp.float32
BF16 = jnp.bfloat16
MESH = pl.DeviceIdType.MESH
DOWN, GATE, UP = 2, 0, 1
ORDER = (DOWN, GATE, UP)


def mm(a, b):
    return jnp.dot(a, b, preferred_element_type=F32)


def mm_nt(a, b):
    return lax.dot_general(a, b, (((1,), (1,)), ((), ())), preferred_element_type=F32)


def mm_tn(a, b):
    return lax.dot_general(a, b, (((0,), (0,)), ((), ())), preferred_element_type=F32)


def orthogonalize(mats):
    xs = []
    for g in mats:
        g = g.astype(F32)
        square = jnp.sum(jnp.sum(g * g, axis=1, keepdims=True), axis=0, keepdims=True)
        xs.append((g / (jnp.sqrt(square) + 1e-07)).astype(BF16))
    for _ in range(NS_STEPS):
        grams = [mm_nt(x, x).astype(BF16) for x in xs]
        mixers = [(coef_b * a.astype(F32) + coef_c * mm(a, a)).astype(BF16) for a in grams]
        xs = [(coef_a * x.astype(F32) + mm(b, x)).astype(BF16) for b, x in zip(mixers, xs)]
    return xs


def kernel(
    sizes, q_hbm, k_hbm, v_hbm, r_hbm, w_hbm, gain_hbm, mixed, wout,
    q0, keys0, vals, w0, rates, gain, dps, kv, qb, act, dgu, hid, w_own, w1, wgu, gd_s, gd_r, gg_s, gg_r, full_d, full_g,
    ysend, ybuf, y0, sq, sqr,
    loc_sem, a2a_s, kv_r, q_r, w_sem, fwd_s, x_s, x_r, c_s, c_r, y_sem, sq_s, sq_r, dist_r, dist_s,
):
    cores, HL, rows, DH = sizes
    width = HL * DH
    half = DH // 2
    core = lax.axis_index("heads")
    t = lax.axis_index("tokens")
    x, y, zl, zh = t % 2, (t // 2) % 2, (t // 4) % 2, t // 8
    z = t // 4
    kind = (x + y + zl) % 2
    home = core == kind
    away = core != kind

    own_slot = x + 2 * y + 4 * zl
    own_head = x + 2 * zl
    mate = t + 8 * (1 - 2 * zh)
    x_near = t + 1 - 2 * x
    y_near = t + 2 * (1 - 2 * y)
    z_near = t + 4 * (1 - 2 * zl)

    def slot(k):
        return (x + k % 2) % 2 + 2 * ((y + k // 2 % 2) % 2) + 4 * ((zl + k // 4) % 2)

    def head_at(dx, dz):
        return (x + dx) % 2 + 2 * ((zl + dz) % 2)

    def owner(dx, dz):
        x0, z0 = (x + dx) % 2, (zl + dz) % 2
        return x0 + 2 * ((x0 + z0 + core) % 2) + 4 * z0 + 8 * zh

    def remote(src, dst, send_sem, recv_sem, device):
        return pltpu.make_async_remote_copy(
            src_ref=src, dst_ref=dst, send_sem=send_sem, recv_sem=recv_sem,
            device_id=device, device_id_type=MESH,
        )

    def send(src, dst, send_sem, recv_sem, device):
        remote(src, dst, send_sem, recv_sem, device).start()

    def arrived(ref, recv_sem):
        remote(ref, ref, loc_sem.at[0], recv_sem, {"tokens": x_near}).wait_recv()

    def drained(ref, send_sem):
        remote(ref, ref, send_sem, loc_sem.at[0], {"tokens": x_near}).wait_send()

    def cols(h):
        return pl.ds(pl.multiple_of(h * DH, DH), DH)

    twin = {"heads": 1 - core}

    local_v = [pltpu.make_async_copy(v_hbm.at[b], vals.at[b], loc_sem.at[4 + b]) for b in range(2)]
    local_r = pltpu.make_async_copy(r_hbm, rates, loc_sem.at[2])
    local_q = pltpu.make_async_copy(q_hbm.at[0], q0, loc_sem.at[0])
    local_w = pltpu.make_async_copy(w_hbm, w0, loc_sem.at[1])
    local_gain = pltpu.make_async_copy(gain_hbm, gain, loc_sem.at[3])
    own_w = pltpu.make_async_copy(w_hbm.at[own_head], w_own, w_sem.at[0])
    local_k = pltpu.make_async_copy(k_hbm.at[0], keys0, loc_sem.at[6])
    local_k.start()
    local_r.start()
    local_v[0].start()
    local_w.start()
    local_q.start()
    local_v[1].start()
    local_gain.start()

    @pl.when(home)
    def _():
        own_w.start()

    barrier = pltpu.get_barrier_semaphore()

    @pl.when(away)
    def _():
        for k in range(8):
            pl.semaphore_signal(
                barrier, inc=1, device_id={"heads": 1 - core, "tokens": slot(k) + 8 * zh}, device_id_type=MESH
            )

    for device in ({"heads": 1 - core}, *({"tokens": chip} for chip in (mate, x_near, y_near, z_near))):
        pl.semaphore_signal(barrier, inc=1, device_id=device, device_id_type=MESH)
    pl.semaphore_wait(barrier, HL + 5)

    def spread(array, view, landing, recv_sems, both=False):
        for dx, dz in SPREAD:
            send(view(head_at(dx, dz)), landing.at[own_slot], a2a_s.at[array], recv_sems.at[own_slot],
                 {"heads": core if both and dz else 1 - core, "tokens": owner(dx, dz)})

    def spread_keys(b):
        spread(2 * b, lambda j: (k_hbm.at[b, :, cols(j)] if b else keys0.at[:, cols(j)]), kv.at[2 * b], kv_r.at[2 * b])

    def spread_values(b):
        spread(2 * b + 1, lambda j: dps.at[b, j], kv.at[2 * b + 1], kv_r.at[2 * b + 1])

    def spread_queries():
        spread(4, lambda j: q_hbm.at[1, :, cols(j)], qb, q_r, both=True)

    def scale_values(b):
        for j in range(HL):
            rate = jnp.broadcast_to(rates[b, pl.ds(j, 1), :], (rows, rows)).T[:, :1]
            dps[b, j] = (rate * vals[b, :, j * DH:(j + 1) * DH].astype(F32)).astype(BF16)

    def issue(point):
        for when, what in zip(ISSUE, (lambda: spread_keys(1), lambda: spread_values(1), spread_queries)):
            if when == point:
                what()

    local_k.wait()
    spread_keys(0)

    @pl.when(home)
    def _():
        send(w_hbm.at[own_head], w_own, fwd_s.at[5], w_sem.at[0], twin)

    local_r.wait()
    local_v[0].wait()
    scale_values(0)
    spread_values(0)
    local_v[1].wait()
    scale_values(1)
    issue(0)

    def share_squares(b, square):
        sq[b] = jnp.broadcast_to(square, (rows, 128))
        send(sq.at[b], sqr.at[b], sq_s.at[b], sq_r.at[b], twin)

    def finish_block(b, read):
        total = sq[b]
        arrived(sqr.at[b], sq_r.at[b])
        total = total + sqr[b]
        root = jnp.sqrt(total[:, :1] / (cores * width) + 1e-06)
        for h in range(HL):
            span = slice(h * DH, (h + 1) * DH)
            mixed[b, :, span] = (read(h) / root * gain[:, span]).astype(BF16)

    def fast_net(rows_in, w_gate, w_up, w_down):
        gate = mm(rows_in, w_gate)
        hidden = (jax.nn.silu(gate) * mm(rows_in, w_up)).astype(BF16)
        return mm(hidden, w_down)

    local_w.wait()
    local_q.wait()
    square = jnp.zeros((rows, 1), F32)
    for h in range(HL):
        span = slice(h * DH, (h + 1) * DH)
        out = fast_net(q0[:, span], w0[h, 0], w0[h, 1], w0[h, 2])
        y0[:, span] = out
        square = square + jnp.sum(out * out, axis=1, keepdims=True)
    share_squares(0, square)

    def halve_weights(w):
        for c in range(2):
            span = slice(c * half, (c + 1) * half)
            wgu[c] = jnp.concatenate([w[GATE, :, span], w[UP, :, span]], axis=1)

    def forward(array, i, when):
        @pl.when(when)
        def _():
            send(kv.at[array, i], kv.at[array, i], fwd_s.at[array], kv_r.at[array, i], twin)

    def gradients(b, w):
        weights = wgu[core]
        w_down = w[DOWN, pl.ds(pl.multiple_of(core * half, half), half), :]
        def activations(i, gate_up, back):
            gate = gate_up[:, :half]
            up = gate_up[:, half:]
            sig = jax.nn.sigmoid(gate)
            hid[i] = (gate * sig * up).astype(BF16)
            dgu[i, :, :half] = (back * up * sig * (1.0 + gate * (1.0 - sig))).astype(BF16)
            dgu[i, :, half:] = (back * gate * sig).astype(BF16)

        if b == 0:
            for k in WAITS:
                i = slot(k)
                arrived(kv.at[0, i], kv_r.at[0, i])
                forward(0, i, away)
                act[k] = mm(kv[0, i], weights)
            for n, k in enumerate(WAITS):
                i = slot(k)
                arrived(kv.at[1, i], kv_r.at[1, i])
                forward(1, i, away)
                activations(i, act[k], mm_nt(kv[1, i], w_down))
                if n == 3:
                    issue(1)
            issue(2)
        else:
            @pl.when(home)
            def _():
                for k in range(8):
                    i = slot(k)
                    arrived(kv.at[2, i], kv_r.at[2, i])
                    arrived(kv.at[3, i], kv_r.at[3, i])

            for i in range(8):
                activations(i, mm(kv[2, i], weights), mm_nt(kv[3, i], w_down))
        count = 8 * rows
        grad = mm_tn(hid[...].reshape(count, half), kv[2 * b + 1].reshape(count, DH))
        gd_s[b] = grad.astype(BF16)
        send(gd_s.at[b], gd_r.at[b], x_s.at[b], x_r.at[b, DOWN], {"tokens": mate})
        grad = mm_tn(kv[2 * b].reshape(count, DH), dgu[...].reshape(count, DH)).astype(BF16)
        gg_s[b, GATE] = grad[:, :half]
        send(gg_s.at[b, GATE], gg_r.at[b, GATE], x_s.at[b], x_r.at[b, GATE], {"tokens": mate})
        gg_s[b, UP] = grad[:, half:]
        send(gg_s.at[b, UP], gg_r.at[b, UP], x_s.at[b], x_r.at[b, UP], {"tokens": mate})

    def exchange(b, m):
        if m == DOWN:
            mine, theirs, full = gd_s.at[b], gd_r.at[b], full_d
        else:
            mine, theirs, full = gg_s.at[b, m], gg_r.at[b, m], full_g.at[m]
        arrived(theirs, x_r.at[b, m])
        total = (mine[...].astype(F32) + theirs[...].astype(F32)).astype(BF16)
        full[b, core] = total
        here = full.at[b, core]
        if b == 0:
            send(here, here, c_s.at[b], c_r.at[b, m], twin)
        else:
            @pl.when(away)
            def _():
                send(here, here, c_s.at[b], c_r.at[b, m], twin)

    def whole(b, m):
        full = full_d if m == DOWN else full_g.at[m]
        arrived(full.at[b, 1 - core], c_r.at[b, m])
        if m == DOWN:
            return full_d[b].reshape(DH, DH)
        return jnp.concatenate([full_g[m, b, 0], full_g[m, b, 1]], axis=1)

    @pl.when(home)
    def _():
        own_w.wait()

    @pl.when(away)
    def _():
        arrived(w_own, w_sem.at[0])

    halve_weights(w_own)
    gradients(0, w_own)
    issue(3)
    local_gain.wait()
    finish_block(0, lambda h: y0[:, h * DH:(h + 1) * DH])
    for m in ORDER:
        exchange(0, m)
    issue(4)

    def pass_on(array):
        @pl.when(away)
        def _():
            for k in range(8):
                i = slot(k)
                arrived(kv.at[array, i], kv_r.at[array, i])
                send(kv.at[array, i], kv.at[array, i], fwd_s.at[array], kv_r.at[array, i], twin)

    if PASS_EARLY >= 1:
        pass_on(2)
    if PASS_EARLY >= 2:
        pass_on(3)
    updates = orthogonalize([whole(0, m) for m in ORDER])
    if PASS_EARLY < 1:
        pass_on(2)
    if PASS_EARLY < 2:
        pass_on(3)
    for m, update in zip(ORDER, updates):
        w1[m] = (w_own[m].astype(F32) + step_size * update.astype(F32)).astype(BF16)
    halve_weights(w1)
    gradients(1, w1)

    def slot_of(k):
        return (own_slot + 4 * home.astype(jnp.int32)) // 4 % 2 * 4 + k

    def new_outputs(first, last):
        for k in range(first, last):
            arrived(qb.at[slot_of(k)], q_r.at[slot_of(k)])
        for k in range(first, last):
            i = slot_of(k)
            ysend[k] = fast_net(qb[i], w1[GATE], w1[UP], w1[DOWN]).astype(BF16)
            send(ysend.at[k], ybuf.at[own_head], y_sem.at[0], y_sem.at[1], {"heads": kind, "tokens": i + 8 * zh})

    def squares_of_block1():
        arrived(ybuf, y_sem.at[1])
        square = jnp.zeros((rows, 1), F32)
        for h in range(HL):
            out = ybuf[h].astype(F32)
            square = square + jnp.sum(out * out, axis=1, keepdims=True)
        share_squares(1, square)

    def rows_of(j, m, which):
        return wout.at[j, m, pl.ds(which * half, half)]

    def wait_part(j, m, which):
        arrived(rows_of(j, m, which), dist_r.at[j, m, which])

    def pass_part(j, m, which, device):
        part = rows_of(j, m, which)
        send(part, part, dist_s.at[0], dist_r.at[j, m, which], {"tokens": device})

    def start_spread(m):
        for which in range(2):
            for chip in (x_near, y_near, z_near):
                pass_part(own_head, m, which, chip)

    def last_step(m):
        @pl.when(home)
        def _():
            (update,) = orthogonalize([whole(1, m)])
            wout[own_head, m] = (w1[m].astype(F32) + step_size * update.astype(F32)).astype(BF16)
            start_spread(m)

    for n, m in enumerate(ORDER):
        new_outputs(CUTS[n], CUTS[n + 1])
        exchange(1, m)
        last_step(m)
    new_outputs(CUTS[3], 4)

    by_x, by_y, by_z = head_at(1, 0), head_at(0, 0), head_at(0, 1)
    opposite = head_at(1, 1)

    def relay(j, m, chip):
        for which in range(2):
            wait_part(j, m, which)
            pass_part(j, m, which, chip)

    @pl.when(away)
    def _():
        first, second, third = ORDER
        relay(by_z, first, y_near)
        relay(by_x, second, z_near)
        relay(by_x, first, z_near)
        relay(by_y, first, x_near)
        squares_of_block1()
        relay(by_y, third, x_near)
        relay(by_y, second, x_near)
        relay(by_z, second, y_near)
        relay(by_x, third, z_near)
        relay(by_z, third, y_near)

    relays = ((by_z, x_near), (opposite, y_near), (by_x, z_near))

    @pl.when(home)
    def _():
        for n, (m, (j, chip)) in enumerate(zip(ORDER, relays)):
            if n == 2:
                squares_of_block1()
            relay(j, m, chip)

    finish_block(1, lambda h: ybuf[h].astype(F32))

    @pl.when(away)
    def _():
        for m in ORDER:
            for which in range(2):
                wait_part(opposite, m, which)

    @pl.when(home)
    def _():
        for m, (relayed, _) in zip(ORDER, relays):
            for j, _ in relays:
                if j is not relayed:
                    for which in range(2):
                        wait_part(j, m, which)

    drained(wout.at[pl.ds(0, 3)], dist_s.at[0])

    @pl.when(home)
    def _():
        drained(wout.at[0], dist_s.at[0])

    for i in range(5):
        drained(qb.at[pl.ds(0, HL)], a2a_s.at[i])

    @pl.when(away)
    def _():
        for i in range(4):
            drained(qb, fwd_s.at[i])
        drained(full_d.at[0], c_s.at[1])
        drained(full_d.at[0, 0], c_s.at[1])

    @pl.when(home)
    def _():
        drained(w_own, fwd_s.at[5])

    for b in range(2):
        drained(full_d.at[0], x_s.at[b])
        drained(full_d.at[0, 0], x_s.at[b])
        drained(sqr.at[b], sq_s.at[b])
    drained(full_d.at[0], c_s.at[0])
    drained(full_d.at[0, 0], c_s.at[0])
    drained(ysend, y_sem.at[0])


WAITS = (0, 7, 3, 5, 6, 1, 2, 4)
SPREAD = ((1, 1), (1, 0), (0, 1), (0, 0))
ISSUE = (0, 1, 4)
PASS_EARLY = 2
CUTS = (0, 4, 4, 4)


def one_kernel(cores, queries, keys, values, rates, fast_init, out_gain):
    blocks, rows, width = queries.shape
    HL, _, DH, _ = fast_init.shape
    half = DH // 2
    dma = lambda *shape: pltpu.SemaphoreType.DMA(shape)
    vm = pltpu.VMEM
    any_space = pl.BlockSpec(memory_space=pl.ANY)
    in_vmem = pl.BlockSpec(memory_space=pltpu.VMEM)
    results = pl.pallas_call(
        functools.partial(kernel, (cores, HL, rows, DH)),
        out_shape=(pltpu.VMEM(queries.shape, BF16), pltpu.VMEM(fast_init.shape, BF16)),
        in_specs=[any_space] * 6,
        out_specs=(in_vmem, in_vmem),
        scratch_shapes=[
            vm((rows, width), BF16),
            vm((rows, width), BF16),
            vm((2, rows, width), BF16),
            vm(fast_init.shape, BF16),
            vm(rates.shape, F32),
            vm((1, width), F32),
            vm((2, HL, rows, DH), BF16),
            vm((4, 8, rows, DH), BF16),
            vm((8, rows, DH), BF16),
            vm((8, rows, DH), F32),
            vm((8, rows, DH), BF16),
            vm((8, rows, half), BF16),
            vm((3, DH, DH), BF16),
            vm((3, DH, DH), BF16),
            vm((2, DH, DH), BF16),
            vm((2, half, DH), BF16),
            vm((2, half, DH), BF16),
            vm((2, 2, DH, half), BF16),
            vm((2, 2, DH, half), BF16),
            vm((2, 2, half, DH), BF16),
            vm((2, 2, 2, DH, half), BF16),
            vm((HL, rows, DH), BF16),
            vm((HL, rows, DH), BF16),
            vm((rows, width), F32),
            vm((2, rows, 128), F32),
            vm((2, rows, 128), F32),
            dma(7),
            dma(5), dma(4, 8), dma(8), dma(1), dma(6),
            dma(2), dma(2, 3), dma(2), dma(2, 3),
            dma(2), dma(2), dma(2),
            dma(4, 3, 2), dma(1),
        ],
        compiler_params=pltpu.CompilerParams(collective_id=0, has_side_effects=True),
    )(queries, keys, values, rates, fast_init, out_gain.reshape(1, width))
    return store(*results)


def store_kernel(mixed, weights, mixed_out, weights_out, sems):
    copies = [pltpu.make_async_copy(mixed.at[b], mixed_out.at[b], sems.at[b]) for b in range(2)]
    copies += [pltpu.make_async_copy(weights.at[h], weights_out.at[h], sems.at[2 + h]) for h in range(weights.shape[0])]
    for copy in copies:
        copy.start()
    for copy in copies:
        copy.wait()


def store(mixed, weights):
    return pl.pallas_call(
        store_kernel,
        out_shape=(jax.ShapeDtypeStruct(mixed.shape, BF16), jax.ShapeDtypeStruct(weights.shape, BF16)),
        in_specs=[pl.BlockSpec(memory_space=pl.ANY)] * 2,
        out_specs=(pl.BlockSpec(memory_space=pltpu.HBM), pl.BlockSpec(memory_space=pltpu.HBM)),
        scratch_shapes=[pltpu.SemaphoreType.DMA((2 + weights.shape[0],))],
    )(*(pltpu.with_memory_space_constraint(a, pltpu.VMEM) for a in (mixed, weights)))


def fits(cores, token_devices, queries, fast_init):
    blocks, rows, width = queries.shape
    HL, _, DH, _ = fast_init.shape
    return (
        blocks == 2 and HL == 4 and cores == 2 and token_devices == 16
        and rows == 128 and DH == 256
    )


def per_device_best(cores, token_devices, queries, keys, values, rates, fast_init, out_gain):
    if fits(cores, token_devices, queries, fast_init):
        return one_kernel(cores, queries, keys, values, rates, fast_init, out_gain)
    return per_device(queries, keys, values, rates, fast_init, out_gain)


def solution(mesh):
    in_specs = (
        P(None, "tokens", "heads"),
        P(None, "tokens", "heads"),
        P(None, "tokens", "heads"),
        P(None, "heads", "tokens"),
        P("heads", None, None, None),
        P("heads"),
    )
    out_specs = (P(None, "tokens", "heads"), P("heads", None, None, None))
    return jax.shard_map(
        functools.partial(per_device_best, mesh.shape["heads"], mesh.shape["tokens"]), mesh=mesh, in_specs=in_specs, out_specs=out_specs, check_vma=False
    )
```

```python
import functools

import jax
import jax.numpy as jnp
from jax import lax
from jax.experimental import pallas as pl
from jax.experimental.pallas import tpu as pltpu
from jax.sharding import PartitionSpec as P

D = 2048
NS_STEPS = 2


coef_a = 3.4445
coef_b = -4.775
coef_c = 2.0315
step_size = 0.5


def newton(current):
    for step in range(NS_STEPS):
        gram = jnp.einsum(
            "hmij,hmkj->hmik", current, current, preferred_element_type=jnp.float32
        ).astype(jnp.bfloat16)
        square = jnp.einsum("hmij,hmjk->hmik", gram, gram, preferred_element_type=jnp.float32)
        mixer = (coef_b * gram.astype(jnp.float32) + coef_c * square).astype(jnp.bfloat16)
        product = jnp.einsum("hmij,hmjk->hmik", mixer, current, preferred_element_type=jnp.float32)
        current = (coef_a * current.astype(jnp.float32) + product).astype(jnp.bfloat16)
    return current


def apply_heads(query, weights):
    gate_q = jnp.einsum("nhd,hde->nhe", query, weights[:, 0], preferred_element_type=jnp.float32)
    up_q = jnp.einsum("nhd,hde->nhe", query, weights[:, 1], preferred_element_type=jnp.float32)
    hidden_q = (jax.nn.silu(gate_q) * up_q).astype(jnp.bfloat16)
    return jnp.einsum("nhd,hde->nhe", hidden_q, weights[:, 2], preferred_element_type=jnp.float32)


def local_grads(key_rows, value_rows, rate, weights):
    gate_k = jnp.einsum("nhd,hde->nhe", key_rows, weights[:, 0], preferred_element_type=jnp.float32)
    up_k = jnp.einsum("nhd,hde->nhe", key_rows, weights[:, 1], preferred_element_type=jnp.float32)
    sig = jax.nn.sigmoid(gate_k)
    hidden = (gate_k * sig * up_k).astype(jnp.bfloat16)
    scaled = (rate.T[:, :, None] * value_rows.astype(jnp.float32)).astype(jnp.bfloat16)
    back = jnp.einsum("nhe,hde->nhd", scaled, weights[:, 2], preferred_element_type=jnp.float32)
    grad_gate = (back * up_k * sig * (1.0 + gate_k * (1.0 - sig))).astype(jnp.bfloat16)
    grad_up = (back * gate_k * sig).astype(jnp.bfloat16)
    g_gate = jnp.einsum("nhd,nhe->hde", key_rows, grad_gate, preferred_element_type=jnp.float32)
    g_up = jnp.einsum("nhd,nhe->hde", key_rows, grad_up, preferred_element_type=jnp.float32)
    g_down = jnp.einsum("nhd,nhe->hde", hidden, scaled, preferred_element_type=jnp.float32)
    return jnp.stack([g_gate, g_up, g_down], axis=1)


def finish(joined, totals, out_gain):
    return (joined / jnp.sqrt(totals[:, None] / D + 1e-06) * out_gain[None, :]).astype(jnp.bfloat16)


def per_device(queries, keys, values, rates, fast_init, out_gain):
    heads_here = fast_init.shape[0]
    head_size = fast_init.shape[2]
    tok_rows = queries.shape[1]
    weights = fast_init
    outputs = []
    joined_all = []
    for block in range(queries.shape[0]):
        query = queries[block].reshape(tok_rows, heads_here, head_size)
        key_rows = keys[block].reshape(tok_rows, heads_here, head_size)
        value_rows = values[block].reshape(tok_rows, heads_here, head_size)
        joined = apply_heads(query, weights).reshape(tok_rows, heads_here * head_size)
        grads = local_grads(key_rows, value_rows, rates[block], weights)
        total = lax.psum(grads, "tokens")
        squares = jnp.sum(total * total, axis=(2, 3))
        start = (total / (jnp.sqrt(squares)[:, :, None, None] + 1e-07)).astype(jnp.bfloat16)
        update = newton(start)
        weights = (weights.astype(jnp.float32) + step_size * update.astype(jnp.float32)).astype(
            jnp.bfloat16
        )
        joined_all.append(joined)
    stacked = jnp.stack(joined_all, axis=0)
    totals = lax.psum(jnp.sum(stacked * stacked, axis=2), "heads")
    outputs = [
        finish(joined_all[index], totals[index], out_gain) for index in range(len(joined_all))
    ]
    return (jnp.stack(outputs, axis=0), weights)


F32 = jnp.float32
BF16 = jnp.bfloat16
MESH = pl.DeviceIdType.MESH
DOWN, GATE, UP = 2, 0, 1
ORDER = (DOWN, GATE, UP)


def mm(a, b):
    return jnp.dot(a, b, preferred_element_type=F32)


def mm_nt(a, b):
    return lax.dot_general(a, b, (((1,), (1,)), ((), ())), preferred_element_type=F32)


def mm_tn(a, b):
    return lax.dot_general(a, b, (((0,), (0,)), ((), ())), preferred_element_type=F32)


def orthogonalize(mats):
    xs = []
    for g in mats:
        g = g.astype(F32)
        square = jnp.sum(jnp.sum(g * g, axis=1, keepdims=True), axis=0, keepdims=True)
        xs.append((g / (jnp.sqrt(square) + 1e-07)).astype(BF16))
    for _ in range(NS_STEPS):
        grams = [mm_nt(x, x).astype(BF16) for x in xs]
        mixers = [(coef_b * a.astype(F32) + coef_c * mm(a, a)).astype(BF16) for a in grams]
        xs = [(coef_a * x.astype(F32) + mm(b, x)).astype(BF16) for b, x in zip(mixers, xs)]
    return xs


def kernel(
    sizes, q_hbm, k_hbm, v_hbm, r_hbm, w_hbm, gain_hbm, mixed, wout,
    q0, keys0, vals, w0, rates, gain, dps, kv, qb, act, dgu, hid, w_own, w1, wgu, gd_s, gd_r, gg_s, gg_r, full_d, full_g,
    ysend, ybuf, y0, sq, sqr,
    loc_sem, a2a_s, kv_r, late_r, q_r, w_sem, fwd_s, x_s, x_r, c_s, c_r, y_sem, sq_s, sq_r, dist_r, dist_s,
):
    cores, HL, rows, DH = sizes
    width = HL * DH
    half = DH // 2
    core = lax.axis_index("heads")
    t = lax.axis_index("tokens")
    x, y, zl, zh = t % 2, (t // 2) % 2, (t // 4) % 2, t // 8
    z = t // 4
    kind = (x + y + zl) % 2
    home = core == kind
    away = core != kind

    own_slot = x + 2 * y + 4 * zl
    own_head = x + 2 * zl
    mate = t + 8 * (1 - 2 * zh)
    x_near = t + 1 - 2 * x
    y_near = t + 2 * (1 - 2 * y)
    z_near = t + 4 * (1 - 2 * zl)

    def slot(k):
        return (x + k % 2) % 2 + 2 * ((y + k // 2 % 2) % 2) + 4 * ((zl + k // 4) % 2)

    def head_at(dx, dz):
        return (x + dx) % 2 + 2 * ((zl + dz) % 2)

    def owner(dx, dz):
        x0, z0 = (x + dx) % 2, (zl + dz) % 2
        return x0 + 2 * ((x0 + z0 + core) % 2) + 4 * z0 + 8 * zh

    def remote(src, dst, send_sem, recv_sem, device):
        return pltpu.make_async_remote_copy(
            src_ref=src, dst_ref=dst, send_sem=send_sem, recv_sem=recv_sem,
            device_id=device, device_id_type=MESH,
        )

    def send(src, dst, send_sem, recv_sem, device):
        remote(src, dst, send_sem, recv_sem, device).start()

    def arrived(ref, recv_sem):
        remote(ref, ref, loc_sem.at[0], recv_sem, {"tokens": x_near}).wait_recv()

    def drained(ref, send_sem):
        remote(ref, ref, send_sem, loc_sem.at[0], {"tokens": x_near}).wait_send()

    def cols(h):
        return pl.ds(pl.multiple_of(h * DH, DH), DH)

    twin = {"heads": 1 - core}

    local_v = [pltpu.make_async_copy(v_hbm.at[b], vals.at[b], loc_sem.at[4 + b]) for b in range(2)]
    local_r = pltpu.make_async_copy(r_hbm, rates, loc_sem.at[2])
    local_q = pltpu.make_async_copy(q_hbm.at[0], q0, loc_sem.at[0])
    local_w = pltpu.make_async_copy(w_hbm, w0, loc_sem.at[1])
    local_gain = pltpu.make_async_copy(gain_hbm, gain, loc_sem.at[3])
    own_w = pltpu.make_async_copy(w_hbm.at[own_head], w_own, w_sem.at[0])
    local_k = pltpu.make_async_copy(k_hbm.at[0], keys0, loc_sem.at[6])
    local_k.start()
    local_r.start()
    local_v[0].start()
    local_w.start()
    local_q.start()
    local_v[1].start()
    local_gain.start()

    @pl.when(home)
    def _():
        own_w.start()

    barrier = pltpu.get_barrier_semaphore()

    @pl.when(away)
    def _():
        for k in range(8):
            pl.semaphore_signal(
                barrier, inc=1, device_id={"heads": 1 - core, "tokens": slot(k) + 8 * zh}, device_id_type=MESH
            )

    for device in ({"heads": 1 - core}, *({"tokens": chip} for chip in (mate, x_near, y_near, z_near))):
        pl.semaphore_signal(barrier, inc=1, device_id=device, device_id_type=MESH)
    pl.semaphore_wait(barrier, HL + 5)

    def spread(array, view, landing, recv_sems, both=False):
        for dx, dz in SPREAD:
            send(view(head_at(dx, dz)), landing.at[own_slot], a2a_s.at[array], recv_sems(own_slot),
                 {"heads": core if both and dz else 1 - core, "tokens": owner(dx, dz)})

    def landed(array):
        return lambda i: kv_r.at[array, i] if array < 2 else late_r.at[array - 2]

    def spread_keys(b):
        spread(2 * b, lambda j: (k_hbm.at[b, :, cols(j)] if b else keys0.at[:, cols(j)]), kv.at[2 * b], landed(2 * b))

    def spread_values(b):
        spread(2 * b + 1, lambda j: dps.at[b, j], kv.at[2 * b + 1], landed(2 * b + 1))

    def spread_queries():
        spread(4, lambda j: q_hbm.at[1, :, cols(j)], qb, lambda i: q_r.at[0], both=True)

    def scale_values(b):
        for j in range(HL):
            rate = jnp.broadcast_to(rates[b, pl.ds(j, 1), :], (rows, rows)).T[:, :1]
            dps[b, j] = (rate * vals[b, :, j * DH:(j + 1) * DH].astype(F32)).astype(BF16)

    def issue(point):
        for when, what in zip(ISSUE, (lambda: spread_keys(1), lambda: spread_values(1), spread_queries)):
            if when == point:
                what()

    local_k.wait()
    spread_keys(0)

    @pl.when(home)
    def _():
        send(w_hbm.at[own_head], w_own, fwd_s.at[5], w_sem.at[0], twin)

    local_r.wait()
    local_v[0].wait()
    scale_values(0)
    spread_values(0)
    local_v[1].wait()
    scale_values(1)

    def share_squares(b, square):
        sq[b] = jnp.broadcast_to(square, (rows, 128))
        send(sq.at[b], sqr.at[b], sq_s.at[b], sq_r.at[b], twin)

    def finish_block(b, read):
        total = sq[b]
        arrived(sqr.at[b], sq_r.at[b])
        total = total + sqr[b]
        root = jnp.sqrt(total[:, :1] / (cores * width) + 1e-06)
        for h in range(HL):
            span = slice(h * DH, (h + 1) * DH)
            mixed[b, :, span] = (read(h) / root * gain[:, span]).astype(BF16)

    def fast_net(rows_in, w_gate, w_up, w_down):
        gate = mm(rows_in, w_gate)
        hidden = (jax.nn.silu(gate) * mm(rows_in, w_up)).astype(BF16)
        return mm(hidden, w_down)

    local_w.wait()
    local_q.wait()
    square = jnp.zeros((rows, 1), F32)
    for h in range(HL):
        span = slice(h * DH, (h + 1) * DH)
        out = fast_net(q0[:, span], w0[h, 0], w0[h, 1], w0[h, 2])
        y0[:, span] = out
        square = square + jnp.sum(out * out, axis=1, keepdims=True)
    share_squares(0, square)

    def halve_weights(w):
        for c in range(2):
            span = slice(c * half, (c + 1) * half)
            wgu[c] = jnp.concatenate([w[GATE, :, span], w[UP, :, span]], axis=1)

    def forward(array, i, when):
        @pl.when(when)
        def _():
            send(kv.at[array, i], kv.at[array, i], fwd_s.at[array], kv_r.at[array, i], twin)

    def gradients(b, w):
        weights = wgu[core]
        w_down = w[DOWN, pl.ds(pl.multiple_of(core * half, half), half), :]
        def activations(i, gate_up, back):
            gate = gate_up[:, :half]
            up = gate_up[:, half:]
            sig = jax.nn.sigmoid(gate)
            hid[i] = (gate * sig * up).astype(BF16)
            dgu[i, :, :half] = (back * up * sig * (1.0 + gate * (1.0 - sig))).astype(BF16)
            dgu[i, :, half:] = (back * gate * sig).astype(BF16)

        if b == 0:
            for n, k in enumerate(WAITS):
                i = slot(k)
                arrived(kv.at[0, i], kv_r.at[0, i])
                forward(0, i, away)
                act[k] = mm(kv[0, i], weights)
                issue(10 + n)
            for n, k in enumerate(WAITS):
                i = slot(k)
                arrived(kv.at[1, i], kv_r.at[1, i])
                forward(1, i, away)
                activations(i, act[k], mm_nt(kv[1, i], w_down))
                issue(20 + n)
        else:
            @pl.when(home)
            def _():
                arrived(kv.at[2], late_r.at[0])
                arrived(kv.at[3], late_r.at[1])

            for i in range(8):
                activations(i, mm(kv[2, i], weights), mm_nt(kv[3, i], w_down))
        count = 8 * rows
        grad = mm_tn(hid[...].reshape(count, half), kv[2 * b + 1].reshape(count, DH))
        gd_s[b] = grad.astype(BF16)
        send(gd_s.at[b], gd_r.at[b], x_s.at[b], x_r.at[b, DOWN], {"tokens": mate})
        grad = mm_tn(kv[2 * b].reshape(count, DH), dgu[...].reshape(count, DH)).astype(BF16)
        gg_s[b, GATE] = grad[:, :half]
        send(gg_s.at[b, GATE], gg_r.at[b, GATE], x_s.at[b], x_r.at[b, GATE], {"tokens": mate})
        gg_s[b, UP] = grad[:, half:]
        send(gg_s.at[b, UP], gg_r.at[b, UP], x_s.at[b], x_r.at[b, UP], {"tokens": mate})

    def exchange(b, m):
        if m == DOWN:
            mine, theirs, full = gd_s.at[b], gd_r.at[b], full_d
        else:
            mine, theirs, full = gg_s.at[b, m], gg_r.at[b, m], full_g.at[m]
        arrived(theirs, x_r.at[b, m])
        total = (mine[...].astype(F32) + theirs[...].astype(F32)).astype(BF16)
        full[b, core] = total
        here = full.at[b, core]
        if b == 0:
            send(here, here, c_s.at[b], c_r.at[b, m], twin)
        else:
            @pl.when(away)
            def _():
                send(here, here, c_s.at[b], c_r.at[b, m], twin)

    def whole(b, m):
        full = full_d if m == DOWN else full_g.at[m]
        arrived(full.at[b, 1 - core], c_r.at[b, m])
        if m == DOWN:
            return full_d[b].reshape(DH, DH)
        return jnp.concatenate([full_g[m, b, 0], full_g[m, b, 1]], axis=1)

    @pl.when(home)
    def _():
        own_w.wait()

    @pl.when(away)
    def _():
        arrived(w_own, w_sem.at[0])

    halve_weights(w_own)
    gradients(0, w_own)
    local_gain.wait()
    finish_block(0, lambda h: y0[:, h * DH:(h + 1) * DH])
    for n, m in enumerate(ORDER):
        exchange(0, m)
        issue(30 + n)

    def pass_on(array):
        @pl.when(away)
        def _():
            arrived(kv.at[array], late_r.at[array - 2])
            send(kv.at[array], kv.at[array], fwd_s.at[array], late_r.at[array - 2], twin)

    if PASS_EARLY >= 1:
        pass_on(2)
    if PASS_EARLY >= 2:
        pass_on(3)
    updates = orthogonalize([whole(0, m) for m in ORDER])
    if PASS_EARLY < 1:
        pass_on(2)
    if PASS_EARLY < 2:
        pass_on(3)
    for m, update in zip(ORDER, updates):
        w1[m] = (w_own[m].astype(F32) + step_size * update.astype(F32)).astype(BF16)
    halve_weights(w1)
    gradients(1, w1)

    def slot_of(k):
        return (own_slot + 4 * home.astype(jnp.int32)) // 4 % 2 * 4 + k

    def new_outputs(first, last):
        if first < last:
            arrived(qb.at[pl.ds(0, 4)], q_r.at[0])
        for k in range(first, last):
            i = slot_of(k)
            ysend[k] = fast_net(qb[i], w1[GATE], w1[UP], w1[DOWN]).astype(BF16)
            send(ysend.at[k], ybuf.at[own_head], y_sem.at[0], y_sem.at[1], {"heads": kind, "tokens": i + 8 * zh})

    def squares_of_block1():
        arrived(ybuf, y_sem.at[1])
        square = jnp.zeros((rows, 1), F32)
        for h in range(HL):
            out = ybuf[h].astype(F32)
            square = square + jnp.sum(out * out, axis=1, keepdims=True)
        share_squares(1, square)

    def rows_of(j, m, which):
        return wout.at[j, m, pl.ds(which * half, half)]

    def wait_part(j, m, which):
        arrived(rows_of(j, m, which), dist_r.at[j, m, which])

    def pass_part(j, m, which, device):
        part = rows_of(j, m, which)
        send(part, part, dist_s.at[0], dist_r.at[j, m, which], {"tokens": device})

    def start_spread(m):
        for which in range(2):
            for chip in (x_near, y_near, z_near):
                pass_part(own_head, m, which, chip)

    def last_step(m):
        @pl.when(home)
        def _():
            (update,) = orthogonalize([whole(1, m)])
            wout[own_head, m] = (w1[m].astype(F32) + step_size * update.astype(F32)).astype(BF16)
            start_spread(m)

    for n, m in enumerate(ORDER):
        new_outputs(CUTS[n], CUTS[n + 1])
        exchange(1, m)
        last_step(m)
    new_outputs(CUTS[3], 4)

    by_x, by_y, by_z = head_at(1, 0), head_at(0, 0), head_at(0, 1)
    opposite = head_at(1, 1)

    def relay(j, m, chip):
        for which in range(2):
            wait_part(j, m, which)
            pass_part(j, m, which, chip)

    @pl.when(away)
    def _():
        first, second, third = ORDER
        relay(by_z, first, y_near)
        relay(by_x, second, z_near)
        relay(by_x, first, z_near)
        relay(by_y, first, x_near)
        squares_of_block1()
        relay(by_y, third, x_near)
        relay(by_y, second, x_near)
        relay(by_z, second, y_near)
        relay(by_x, third, z_near)
        relay(by_z, third, y_near)

    relays = ((by_z, x_near), (opposite, y_near), (by_x, z_near))

    @pl.when(home)
    def _():
        for n, (m, (j, chip)) in enumerate(zip(ORDER, relays)):
            if n == 2:
                squares_of_block1()
            relay(j, m, chip)

    finish_block(1, lambda h: ybuf[h].astype(F32))

    @pl.when(away)
    def _():
        for m in ORDER:
            for which in range(2):
                wait_part(opposite, m, which)

    @pl.when(home)
    def _():
        for m, (relayed, _) in zip(ORDER, relays):
            for j, _ in relays:
                if j is not relayed:
                    for which in range(2):
                        wait_part(j, m, which)

    drained(wout.at[pl.ds(0, 3)], dist_s.at[0])

    @pl.when(home)
    def _():
        drained(wout.at[0], dist_s.at[0])

    for i in range(5):
        drained(qb.at[pl.ds(0, HL)], a2a_s.at[i])

    @pl.when(away)
    def _():
        for i in range(4):
            drained(qb, fwd_s.at[i])
        drained(full_d.at[0], c_s.at[1])
        drained(full_d.at[0, 0], c_s.at[1])

    @pl.when(home)
    def _():
        drained(w_own, fwd_s.at[5])

    for b in range(2):
        drained(full_d.at[0], x_s.at[b])
        drained(full_d.at[0, 0], x_s.at[b])
        drained(sqr.at[b], sq_s.at[b])
    drained(full_d.at[0], c_s.at[0])
    drained(full_d.at[0, 0], c_s.at[0])
    drained(ysend, y_sem.at[0])


WAITS = (0, 7, 3, 5, 6, 1, 2, 4)
SPREAD = ((1, 1), (1, 0), (0, 1), (0, 0))
ISSUE = (11, 23, 32)
PASS_EARLY = 2
CUTS = (0, 4, 4, 4)


def one_kernel(cores, queries, keys, values, rates, fast_init, out_gain):
    blocks, rows, width = queries.shape
    HL, _, DH, _ = fast_init.shape
    half = DH // 2
    dma = lambda *shape: pltpu.SemaphoreType.DMA(shape)
    vm = pltpu.VMEM
    any_space = pl.BlockSpec(memory_space=pl.ANY)
    in_vmem = pl.BlockSpec(memory_space=pltpu.VMEM)
    results = pl.pallas_call(
        functools.partial(kernel, (cores, HL, rows, DH)),
        out_shape=(pltpu.VMEM(queries.shape, BF16), pltpu.VMEM(fast_init.shape, BF16)),
        in_specs=[any_space] * 6,
        out_specs=(in_vmem, in_vmem),
        scratch_shapes=[
            vm((rows, width), BF16),
            vm((rows, width), BF16),
            vm((2, rows, width), BF16),
            vm(fast_init.shape, BF16),
            vm(rates.shape, F32),
            vm((1, width), F32),
            vm((2, HL, rows, DH), BF16),
            vm((4, 8, rows, DH), BF16),
            vm((8, rows, DH), BF16),
            vm((8, rows, DH), F32),
            vm((8, rows, DH), BF16),
            vm((8, rows, half), BF16),
            vm((3, DH, DH), BF16),
            vm((3, DH, DH), BF16),
            vm((2, DH, DH), BF16),
            vm((2, half, DH), BF16),
            vm((2, half, DH), BF16),
            vm((2, 2, DH, half), BF16),
            vm((2, 2, DH, half), BF16),
            vm((2, 2, half, DH), BF16),
            vm((2, 2, 2, DH, half), BF16),
            vm((HL, rows, DH), BF16),
            vm((HL, rows, DH), BF16),
            vm((rows, width), F32),
            vm((2, rows, 128), F32),
            vm((2, rows, 128), F32),
            dma(7),
            dma(5), dma(2, 8), dma(2), dma(1), dma(1), dma(6),
            dma(2), dma(2, 3), dma(2), dma(2, 3),
            dma(2), dma(2), dma(2),
            dma(4, 3, 2), dma(1),
        ],
        compiler_params=pltpu.CompilerParams(collective_id=0, has_side_effects=True),
    )(queries, keys, values, rates, fast_init, out_gain.reshape(1, width))
    return store(*results)


def store_kernel(mixed, weights, mixed_out, weights_out, sems):
    copies = [pltpu.make_async_copy(mixed.at[b], mixed_out.at[b], sems.at[b]) for b in range(2)]
    copies += [pltpu.make_async_copy(weights.at[h], weights_out.at[h], sems.at[2 + h]) for h in range(weights.shape[0])]
    for copy in copies:
        copy.start()
    for copy in copies:
        copy.wait()


def store(mixed, weights):
    return pl.pallas_call(
        store_kernel,
        out_shape=(jax.ShapeDtypeStruct(mixed.shape, BF16), jax.ShapeDtypeStruct(weights.shape, BF16)),
        in_specs=[pl.BlockSpec(memory_space=pl.ANY)] * 2,
        out_specs=(pl.BlockSpec(memory_space=pltpu.HBM), pl.BlockSpec(memory_space=pltpu.HBM)),
        scratch_shapes=[pltpu.SemaphoreType.DMA((2 + weights.shape[0],))],
    )(*(pltpu.with_memory_space_constraint(a, pltpu.VMEM) for a in (mixed, weights)))


def fits(cores, token_devices, queries, fast_init):
    blocks, rows, width = queries.shape
    HL, _, DH, _ = fast_init.shape
    return (
        blocks == 2 and HL == 4 and cores == 2 and token_devices == 16
        and rows == 128 and DH == 256
    )


def per_device_best(cores, token_devices, queries, keys, values, rates, fast_init, out_gain):
    if fits(cores, token_devices, queries, fast_init):
        return one_kernel(cores, queries, keys, values, rates, fast_init, out_gain)
    return per_device(queries, keys, values, rates, fast_init, out_gain)


def solution(mesh):
    in_specs = (
        P(None, "tokens", "heads"),
        P(None, "tokens", "heads"),
        P(None, "tokens", "heads"),
        P(None, "heads", "tokens"),
        P("heads", None, None, None),
        P("heads"),
    )
    out_specs = (P(None, "tokens", "heads"), P("heads", None, None, None))
    return jax.shard_map(
        functools.partial(per_device_best, mesh.shape["heads"], mesh.shape["tokens"]), mesh=mesh, in_specs=in_specs, out_specs=out_specs, check_vma=False
    )
```

```python
import functools

import jax
import jax.numpy as jnp
from jax import lax
from jax.experimental import pallas as pl
from jax.experimental.pallas import tpu as pltpu
from jax.sharding import PartitionSpec as P

D = 2048
NS_STEPS = 2


coef_a = 3.4445
coef_b = -4.775
coef_c = 2.0315
step_size = 0.5


def newton(current):
    for step in range(NS_STEPS):
        gram = jnp.einsum(
            "hmij,hmkj->hmik", current, current, preferred_element_type=jnp.float32
        ).astype(jnp.bfloat16)
        square = jnp.einsum("hmij,hmjk->hmik", gram, gram, preferred_element_type=jnp.float32)
        mixer = (coef_b * gram.astype(jnp.float32) + coef_c * square).astype(jnp.bfloat16)
        product = jnp.einsum("hmij,hmjk->hmik", mixer, current, preferred_element_type=jnp.float32)
        current = (coef_a * current.astype(jnp.float32) + product).astype(jnp.bfloat16)
    return current


def apply_heads(query, weights):
    gate_q = jnp.einsum("nhd,hde->nhe", query, weights[:, 0], preferred_element_type=jnp.float32)
    up_q = jnp.einsum("nhd,hde->nhe", query, weights[:, 1], preferred_element_type=jnp.float32)
    hidden_q = (jax.nn.silu(gate_q) * up_q).astype(jnp.bfloat16)
    return jnp.einsum("nhd,hde->nhe", hidden_q, weights[:, 2], preferred_element_type=jnp.float32)


def local_grads(key_rows, value_rows, rate, weights):
    gate_k = jnp.einsum("nhd,hde->nhe", key_rows, weights[:, 0], preferred_element_type=jnp.float32)
    up_k = jnp.einsum("nhd,hde->nhe", key_rows, weights[:, 1], preferred_element_type=jnp.float32)
    sig = jax.nn.sigmoid(gate_k)
    hidden = (gate_k * sig * up_k).astype(jnp.bfloat16)
    scaled = (rate.T[:, :, None] * value_rows.astype(jnp.float32)).astype(jnp.bfloat16)
    back = jnp.einsum("nhe,hde->nhd", scaled, weights[:, 2], preferred_element_type=jnp.float32)
    grad_gate = (back * up_k * sig * (1.0 + gate_k * (1.0 - sig))).astype(jnp.bfloat16)
    grad_up = (back * gate_k * sig).astype(jnp.bfloat16)
    g_gate = jnp.einsum("nhd,nhe->hde", key_rows, grad_gate, preferred_element_type=jnp.float32)
    g_up = jnp.einsum("nhd,nhe->hde", key_rows, grad_up, preferred_element_type=jnp.float32)
    g_down = jnp.einsum("nhd,nhe->hde", hidden, scaled, preferred_element_type=jnp.float32)
    return jnp.stack([g_gate, g_up, g_down], axis=1)


def finish(joined, totals, out_gain):
    return (joined / jnp.sqrt(totals[:, None] / D + 1e-06) * out_gain[None, :]).astype(jnp.bfloat16)


def per_device(queries, keys, values, rates, fast_init, out_gain):
    heads_here = fast_init.shape[0]
    head_size = fast_init.shape[2]
    tok_rows = queries.shape[1]
    weights = fast_init
    outputs = []
    joined_all = []
    for block in range(queries.shape[0]):
        query = queries[block].reshape(tok_rows, heads_here, head_size)
        key_rows = keys[block].reshape(tok_rows, heads_here, head_size)
        value_rows = values[block].reshape(tok_rows, heads_here, head_size)
        joined = apply_heads(query, weights).reshape(tok_rows, heads_here * head_size)
        grads = local_grads(key_rows, value_rows, rates[block], weights)
        total = lax.psum(grads, "tokens")
        squares = jnp.sum(total * total, axis=(2, 3))
        start = (total / (jnp.sqrt(squares)[:, :, None, None] + 1e-07)).astype(jnp.bfloat16)
        update = newton(start)
        weights = (weights.astype(jnp.float32) + step_size * update.astype(jnp.float32)).astype(
            jnp.bfloat16
        )
        joined_all.append(joined)
    stacked = jnp.stack(joined_all, axis=0)
    totals = lax.psum(jnp.sum(stacked * stacked, axis=2), "heads")
    outputs = [
        finish(joined_all[index], totals[index], out_gain) for index in range(len(joined_all))
    ]
    return (jnp.stack(outputs, axis=0), weights)


F32 = jnp.float32
BF16 = jnp.bfloat16
MESH = pl.DeviceIdType.MESH
DOWN, GATE, UP = 2, 0, 1
ORDER = (DOWN, GATE, UP)


def mm(a, b):
    return jnp.dot(a, b, preferred_element_type=F32)


def mm_nt(a, b):
    return lax.dot_general(a, b, (((1,), (1,)), ((), ())), preferred_element_type=F32)


def mm_tn(a, b):
    return lax.dot_general(a, b, (((0,), (0,)), ((), ())), preferred_element_type=F32)


def orthogonalize(mats):
    xs = []
    for g in mats:
        g = g.astype(F32)
        square = jnp.sum(jnp.sum(g * g, axis=1, keepdims=True), axis=0, keepdims=True)
        xs.append((g / (jnp.sqrt(square) + 1e-07)).astype(BF16))
    for _ in range(NS_STEPS):
        grams = [mm_nt(x, x).astype(BF16) for x in xs]
        mixers = [(coef_b * a.astype(F32) + coef_c * mm(a, a)).astype(BF16) for a in grams]
        xs = [(coef_a * x.astype(F32) + mm(b, x)).astype(BF16) for b, x in zip(mixers, xs)]
    return xs


def kernel(
    sizes, q_hbm, k_hbm, v_hbm, r_hbm, w_hbm, gain_hbm, mixed, wout,
    q0, keys0, vals, w0, rates, gain, dps, kv, qb, act, dgu, hid, w_own, w1, wgu, gd_s, gd_r, gg_s, gg_r, full_d, full_g,
    ysend, ybuf, y0, sq, sqr,
    loc_sem, a2a_s, kv_r, late_r, q_r, w_sem, fwd_s, x_s, x_r, c_s, c_r, y_sem, sq_s, sq_r, dist_r, dist_s,
):
    cores, HL, rows, DH = sizes
    width = HL * DH
    half = DH // 2
    core = lax.axis_index("heads")
    t = lax.axis_index("tokens")
    x, y, zl, zh = t % 2, (t // 2) % 2, (t // 4) % 2, t // 8
    z = t // 4
    kind = (x + y + zl) % 2
    home = core == kind
    away = core != kind

    own_slot = x + 2 * y + 4 * zl
    own_head = x + 2 * zl
    mate = t + 8 * (1 - 2 * zh)
    x_near = t + 1 - 2 * x
    y_near = t + 2 * (1 - 2 * y)
    z_near = t + 4 * (1 - 2 * zl)

    def slot(k):
        return (x + k % 2) % 2 + 2 * ((y + k // 2 % 2) % 2) + 4 * ((zl + k // 4) % 2)

    def head_at(dx, dz):
        return (x + dx) % 2 + 2 * ((zl + dz) % 2)

    def owner(dx, dz):
        x0, z0 = (x + dx) % 2, (zl + dz) % 2
        return x0 + 2 * ((x0 + z0 + core) % 2) + 4 * z0 + 8 * zh

    def remote(src, dst, send_sem, recv_sem, device):
        return pltpu.make_async_remote_copy(
            src_ref=src, dst_ref=dst, send_sem=send_sem, recv_sem=recv_sem,
            device_id=device, device_id_type=MESH,
        )

    def send(src, dst, send_sem, recv_sem, device):
        remote(src, dst, send_sem, recv_sem, device).start()

    def arrived(ref, recv_sem):
        remote(ref, ref, loc_sem.at[0], recv_sem, {"tokens": x_near}).wait_recv()

    def drained(ref, send_sem):
        remote(ref, ref, send_sem, loc_sem.at[0], {"tokens": x_near}).wait_send()

    def cols(h):
        return pl.ds(pl.multiple_of(h * DH, DH), DH)

    twin = {"heads": 1 - core}

    local_v = [pltpu.make_async_copy(v_hbm.at[b], vals.at[b], loc_sem.at[4 + b]) for b in range(2)]
    local_r = pltpu.make_async_copy(r_hbm, rates, loc_sem.at[2])
    local_q = pltpu.make_async_copy(q_hbm.at[0], q0, loc_sem.at[0])
    local_w = pltpu.make_async_copy(w_hbm, w0, loc_sem.at[1])
    local_gain = pltpu.make_async_copy(gain_hbm, gain, loc_sem.at[3])
    own_w = pltpu.make_async_copy(w_hbm.at[own_head], w_own, w_sem.at[0])
    local_k = pltpu.make_async_copy(k_hbm.at[0], keys0, loc_sem.at[6])
    local_k.start()
    local_r.start()
    local_v[0].start()
    local_w.start()
    local_q.start()
    local_v[1].start()
    local_gain.start()

    @pl.when(home)
    def _():
        own_w.start()

    barrier = pltpu.get_barrier_semaphore()

    @pl.when(away)
    def _():
        for k in range(8):
            pl.semaphore_signal(
                barrier, inc=1, device_id={"heads": 1 - core, "tokens": slot(k) + 8 * zh}, device_id_type=MESH
            )

    for device in ({"heads": 1 - core}, *({"tokens": chip} for chip in (mate, x_near, y_near, z_near))):
        pl.semaphore_signal(barrier, inc=1, device_id=device, device_id_type=MESH)
    pl.semaphore_wait(barrier, HL + 5)

    def spread(array, view, landing, recv_sems, both=False):
        for dx, dz in SPREAD:
            send(view(head_at(dx, dz)), landing.at[own_slot], a2a_s.at[array], recv_sems(own_slot),
                 {"heads": core if both and dz else 1 - core, "tokens": owner(dx, dz)})

    def landed(array):
        return lambda i: kv_r.at[array, i] if array < 2 else late_r.at[array - 2]

    def spread_keys(b):
        spread(2 * b, lambda j: (k_hbm.at[b, :, cols(j)] if b else keys0.at[:, cols(j)]), kv.at[2 * b], landed(2 * b))

    def spread_values(b):
        spread(2 * b + 1, lambda j: dps.at[b, j], kv.at[2 * b + 1], landed(2 * b + 1))

    def spread_queries():
        spread(4, lambda j: q_hbm.at[1, :, cols(j)], qb, lambda i: q_r.at[0], both=True)

    def scale_values(b):
        for j in range(HL):
            rate = jnp.broadcast_to(rates[b, pl.ds(j, 1), :], (rows, rows)).T[:, :1]
            dps[b, j] = (rate * vals[b, :, j * DH:(j + 1) * DH].astype(F32)).astype(BF16)

    def issue(point):
        for when, what in zip(ISSUE, (lambda: spread_keys(1), lambda: spread_values(1), spread_queries)):
            if when == point:
                what()

    local_k.wait()
    spread_keys(0)

    @pl.when(home)
    def _():
        send(w_hbm.at[own_head], w_own, fwd_s.at[5], w_sem.at[0], twin)

    local_r.wait()
    local_v[0].wait()
    scale_values(0)
    spread_values(0)
    local_v[1].wait()
    scale_values(1)

    def share_squares(b, square):
        sq[b] = jnp.broadcast_to(square, (rows, 128))
        send(sq.at[b], sqr.at[b], sq_s.at[b], sq_r.at[b], twin)

    def finish_block(b, read):
        total = sq[b]
        arrived(sqr.at[b], sq_r.at[b])
        total = total + sqr[b]
        root = jnp.sqrt(total[:, :1] / (cores * width) + 1e-06)
        for h in range(HL):
            span = slice(h * DH, (h + 1) * DH)
            mixed[b, :, span] = (read(h) / root * gain[:, span]).astype(BF16)

    def fast_net(rows_in, w_gate, w_up, w_down):
        gate = mm(rows_in, w_gate)
        hidden = (jax.nn.silu(gate) * mm(rows_in, w_up)).astype(BF16)
        return mm(hidden, w_down)

    local_w.wait()
    local_q.wait()
    square = jnp.zeros((rows, 1), F32)
    for h in range(HL):
        span = slice(h * DH, (h + 1) * DH)
        out = fast_net(q0[:, span], w0[h, 0], w0[h, 1], w0[h, 2])
        y0[:, span] = out
        square = square + jnp.sum(out * out, axis=1, keepdims=True)
    share_squares(0, square)

    def halve_weights(w):
        for c in range(2):
            span = slice(c * half, (c + 1) * half)
            wgu[c] = jnp.concatenate([w[GATE, :, span], w[UP, :, span]], axis=1)

    def forward(array, i, when):
        @pl.when(when)
        def _():
            send(kv.at[array, i], kv.at[array, i], fwd_s.at[array], kv_r.at[array, i], twin)

    def gradients(b, w):
        weights = wgu[core]
        w_down = w[DOWN, pl.ds(pl.multiple_of(core * half, half), half), :]
        def activations(i, gate_up, back):
            gate = gate_up[:, :half]
            up = gate_up[:, half:]
            sig = jax.nn.sigmoid(gate)
            hid[i] = (gate * sig * up).astype(BF16)
            dgu[i, :, :half] = (back * up * sig * (1.0 + gate * (1.0 - sig))).astype(BF16)
            dgu[i, :, half:] = (back * gate * sig).astype(BF16)

        if b == 0:
            for n, k in enumerate(WAITS):
                i = slot(k)
                arrived(kv.at[0, i], kv_r.at[0, i])
                forward(0, i, away)
                act[k] = mm(kv[0, i], weights)
                issue(10 + n)
            for n, k in enumerate(WAITS):
                i = slot(k)
                arrived(kv.at[1, i], kv_r.at[1, i])
                forward(1, i, away)
                activations(i, act[k], mm_nt(kv[1, i], w_down))
                issue(20 + n)
        else:
            @pl.when(home)
            def _():
                arrived(kv.at[2], late_r.at[0])
                arrived(kv.at[3], late_r.at[1])

            for i in range(8):
                activations(i, mm(kv[2, i], weights), mm_nt(kv[3, i], w_down))
        count = 8 * rows
        grad = mm_tn(hid[...].reshape(count, half), kv[2 * b + 1].reshape(count, DH))
        gd_s[b] = grad.astype(BF16)
        send(gd_s.at[b], gd_r.at[b], x_s.at[b], x_r.at[b, DOWN], {"tokens": mate})
        grad = mm_tn(kv[2 * b].reshape(count, DH), dgu[...].reshape(count, DH)).astype(BF16)
        gg_s[b, GATE] = grad[:, :half]
        send(gg_s.at[b, GATE], gg_r.at[b, GATE], x_s.at[b], x_r.at[b, GATE], {"tokens": mate})
        gg_s[b, UP] = grad[:, half:]
        send(gg_s.at[b, UP], gg_r.at[b, UP], x_s.at[b], x_r.at[b, UP], {"tokens": mate})

    def exchange(b, m):
        if m == DOWN:
            mine, theirs, full = gd_s.at[b], gd_r.at[b], full_d
        else:
            mine, theirs, full = gg_s.at[b, m], gg_r.at[b, m], full_g.at[m]
        arrived(theirs, x_r.at[b, m])
        total = (mine[...].astype(F32) + theirs[...].astype(F32)).astype(BF16)
        full[b, core] = total
        here = full.at[b, core]
        if b == 0:
            send(here, here, c_s.at[b], c_r.at[b, m], twin)
        else:
            @pl.when(away)
            def _():
                send(here, here, c_s.at[b], c_r.at[b, m], twin)

    def whole(b, m):
        full = full_d if m == DOWN else full_g.at[m]
        arrived(full.at[b, 1 - core], c_r.at[b, m])
        if m == DOWN:
            return full_d[b].reshape(DH, DH)
        return jnp.concatenate([full_g[m, b, 0], full_g[m, b, 1]], axis=1)

    @pl.when(home)
    def _():
        own_w.wait()

    @pl.when(away)
    def _():
        arrived(w_own, w_sem.at[0])

    halve_weights(w_own)
    gradients(0, w_own)
    local_gain.wait()
    finish_block(0, lambda h: y0[:, h * DH:(h + 1) * DH])
    for n, m in enumerate(ORDER):
        exchange(0, m)
        issue(30 + n)

    def pass_on(array):
        @pl.when(away)
        def _():
            arrived(kv.at[array], late_r.at[array - 2])
            send(kv.at[array], kv.at[array], fwd_s.at[array], late_r.at[array - 2], twin)

    if PASS_EARLY >= 1:
        pass_on(2)
    if PASS_EARLY >= 2:
        pass_on(3)
    updates = orthogonalize([whole(0, m) for m in ORDER])
    if PASS_EARLY < 1:
        pass_on(2)
    if PASS_EARLY < 2:
        pass_on(3)
    for m, update in zip(ORDER, updates):
        w1[m] = (w_own[m].astype(F32) + step_size * update.astype(F32)).astype(BF16)
    halve_weights(w1)
    gradients(1, w1)

    def slot_of(k):
        return (own_slot + 4 * home.astype(jnp.int32)) // 4 % 2 * 4 + k

    def new_outputs(first, last):
        if first < last:
            arrived(qb.at[pl.ds(0, 4)], q_r.at[0])
        for k in range(first, last):
            i = slot_of(k)
            ysend[k] = fast_net(qb[i], w1[GATE], w1[UP], w1[DOWN]).astype(BF16)
            send(ysend.at[k], ybuf.at[own_head], y_sem.at[0], y_sem.at[1], {"heads": kind, "tokens": i + 8 * zh})

    def squares_of_block1():
        arrived(ybuf, y_sem.at[1])
        square = jnp.zeros((rows, 1), F32)
        for h in range(HL):
            out = ybuf[h].astype(F32)
            square = square + jnp.sum(out * out, axis=1, keepdims=True)
        share_squares(1, square)

    def rows_of(j, m, which):
        return wout.at[j, m, pl.ds(which * half, half)]

    def wait_part(j, m, which):
        arrived(rows_of(j, m, which), dist_r.at[j, m, which])

    def pass_part(j, m, which, device):
        part = rows_of(j, m, which)
        send(part, part, dist_s.at[0], dist_r.at[j, m, which], {"tokens": device})

    def start_spread(m):
        for which in range(2):
            for chip in (x_near, y_near, z_near):
                pass_part(own_head, m, which, chip)

    def last_step(m):
        @pl.when(home)
        def _():
            (update,) = orthogonalize([whole(1, m)])
            wout[own_head, m] = (w1[m].astype(F32) + step_size * update.astype(F32)).astype(BF16)
            start_spread(m)

    for n, m in enumerate(ORDER):
        new_outputs(CUTS[n], CUTS[n + 1])
        exchange(1, m)
        last_step(m)
    new_outputs(CUTS[3], 4)

    by_x, by_y, by_z = head_at(1, 0), head_at(0, 0), head_at(0, 1)
    opposite = head_at(1, 1)

    def relay(j, m, chip):
        for which in range(2):
            wait_part(j, m, which)
            pass_part(j, m, which, chip)

    @pl.when(away)
    def _():
        first, second, third = ORDER
        relay(by_z, first, y_near)
        relay(by_x, second, z_near)
        relay(by_x, first, z_near)
        relay(by_y, first, x_near)
        squares_of_block1()
        relay(by_y, third, x_near)
        relay(by_y, second, x_near)
        relay(by_z, second, y_near)
        relay(by_x, third, z_near)
        relay(by_z, third, y_near)

    relays = ((by_z, x_near), (opposite, y_near), (by_x, z_near))

    @pl.when(home)
    def _():
        for n, (m, (j, chip)) in enumerate(zip(ORDER, relays)):
            if n == 2:
                squares_of_block1()
            relay(j, m, chip)

    finish_block(1, lambda h: ybuf[h].astype(F32))

    @pl.when(away)
    def _():
        for m in ORDER:
            for which in range(2):
                wait_part(opposite, m, which)

    @pl.when(home)
    def _():
        for m, (relayed, _) in zip(ORDER, relays):
            for j, _ in relays:
                if j is not relayed:
                    for which in range(2):
                        wait_part(j, m, which)

    drained(wout.at[pl.ds(0, 3)], dist_s.at[0])

    @pl.when(home)
    def _():
        drained(wout.at[0], dist_s.at[0])

    for i in range(5):
        drained(qb.at[pl.ds(0, HL)], a2a_s.at[i])

    @pl.when(away)
    def _():
        for i in range(4):
            drained(qb, fwd_s.at[i])
        drained(full_d.at[0], c_s.at[1])
        drained(full_d.at[0, 0], c_s.at[1])

    @pl.when(home)
    def _():
        drained(w_own, fwd_s.at[5])

    for b in range(2):
        drained(full_d.at[0], x_s.at[b])
        drained(full_d.at[0, 0], x_s.at[b])
        drained(sqr.at[b], sq_s.at[b])
    drained(full_d.at[0], c_s.at[0])
    drained(full_d.at[0, 0], c_s.at[0])
    drained(ysend, y_sem.at[0])


WAITS = (0, 7, 3, 5, 6, 1, 2, 4)
SPREAD = ((1, 1), (0, 1), (1, 0), (0, 0))
ISSUE = (10, 23, 32)
PASS_EARLY = 2
CUTS = (0, 4, 4, 4)


def one_kernel(cores, queries, keys, values, rates, fast_init, out_gain):
    blocks, rows, width = queries.shape
    HL, _, DH, _ = fast_init.shape
    half = DH // 2
    dma = lambda *shape: pltpu.SemaphoreType.DMA(shape)
    vm = pltpu.VMEM
    any_space = pl.BlockSpec(memory_space=pl.ANY)
    in_vmem = pl.BlockSpec(memory_space=pltpu.VMEM)
    results = pl.pallas_call(
        functools.partial(kernel, (cores, HL, rows, DH)),
        out_shape=(pltpu.VMEM(queries.shape, BF16), pltpu.VMEM(fast_init.shape, BF16)),
        in_specs=[any_space] * 6,
        out_specs=(in_vmem, in_vmem),
        scratch_shapes=[
            vm((rows, width), BF16),
            vm((rows, width), BF16),
            vm((2, rows, width), BF16),
            vm(fast_init.shape, BF16),
            vm(rates.shape, F32),
            vm((1, width), F32),
            vm((2, HL, rows, DH), BF16),
            vm((4, 8, rows, DH), BF16),
            vm((8, rows, DH), BF16),
            vm((8, rows, DH), F32),
            vm((8, rows, DH), BF16),
            vm((8, rows, half), BF16),
            vm((3, DH, DH), BF16),
            vm((3, DH, DH), BF16),
            vm((2, DH, DH), BF16),
            vm((2, half, DH), BF16),
            vm((2, half, DH), BF16),
            vm((2, 2, DH, half), BF16),
            vm((2, 2, DH, half), BF16),
            vm((2, 2, half, DH), BF16),
            vm((2, 2, 2, DH, half), BF16),
            vm((HL, rows, DH), BF16),
            vm((HL, rows, DH), BF16),
            vm((rows, width), F32),
            vm((2, rows, 128), F32),
            vm((2, rows, 128), F32),
            dma(7),
            dma(5), dma(2, 8), dma(2), dma(1), dma(1), dma(6),
            dma(2), dma(2, 3), dma(2), dma(2, 3),
            dma(2), dma(2), dma(2),
            dma(4, 3, 2), dma(1),
        ],
        compiler_params=pltpu.CompilerParams(collective_id=0, has_side_effects=True),
    )(queries, keys, values, rates, fast_init, out_gain.reshape(1, width))
    return store(*results)


def store_kernel(mixed, weights, mixed_out, weights_out, sems):
    copies = [pltpu.make_async_copy(mixed.at[b], mixed_out.at[b], sems.at[b]) for b in range(2)]
    copies += [pltpu.make_async_copy(weights.at[h], weights_out.at[h], sems.at[2 + h]) for h in range(weights.shape[0])]
    for copy in copies:
        copy.start()
    for copy in copies:
        copy.wait()


def store(mixed, weights):
    return pl.pallas_call(
        store_kernel,
        out_shape=(jax.ShapeDtypeStruct(mixed.shape, BF16), jax.ShapeDtypeStruct(weights.shape, BF16)),
        in_specs=[pl.BlockSpec(memory_space=pl.ANY)] * 2,
        out_specs=(pl.BlockSpec(memory_space=pltpu.HBM), pl.BlockSpec(memory_space=pltpu.HBM)),
        scratch_shapes=[pltpu.SemaphoreType.DMA((2 + weights.shape[0],))],
    )(*(pltpu.with_memory_space_constraint(a, pltpu.VMEM) for a in (mixed, weights)))


def fits(cores, token_devices, queries, fast_init):
    blocks, rows, width = queries.shape
    HL, _, DH, _ = fast_init.shape
    return (
        blocks == 2 and HL == 4 and cores == 2 and token_devices == 16
        and rows == 128 and DH == 256
    )


def per_device_best(cores, token_devices, queries, keys, values, rates, fast_init, out_gain):
    if fits(cores, token_devices, queries, fast_init):
        return one_kernel(cores, queries, keys, values, rates, fast_init, out_gain)
    return per_device(queries, keys, values, rates, fast_init, out_gain)


def solution(mesh):
    in_specs = (
        P(None, "tokens", "heads"),
        P(None, "tokens", "heads"),
        P(None, "tokens", "heads"),
        P(None, "heads", "tokens"),
        P("heads", None, None, None),
        P("heads"),
    )
    out_specs = (P(None, "tokens", "heads"), P("heads", None, None, None))
    return jax.shard_map(
        functools.partial(per_device_best, mesh.shape["heads"], mesh.shape["tokens"]), mesh=mesh, in_specs=in_specs, out_specs=out_specs, check_vma=False
    )
```

```python
import functools

import jax
import jax.numpy as jnp
from jax import lax
from jax.experimental import pallas as pl
from jax.experimental.pallas import tpu as pltpu
from jax.sharding import PartitionSpec as P

D = 2048
NS_STEPS = 2


coef_a = 3.4445
coef_b = -4.775
coef_c = 2.0315
step_size = 0.5


def newton(current):
    for step in range(NS_STEPS):
        gram = jnp.einsum(
            "hmij,hmkj->hmik", current, current, preferred_element_type=jnp.float32
        ).astype(jnp.bfloat16)
        square = jnp.einsum("hmij,hmjk->hmik", gram, gram, preferred_element_type=jnp.float32)
        mixer = (coef_b * gram.astype(jnp.float32) + coef_c * square).astype(jnp.bfloat16)
        product = jnp.einsum("hmij,hmjk->hmik", mixer, current, preferred_element_type=jnp.float32)
        current = (coef_a * current.astype(jnp.float32) + product).astype(jnp.bfloat16)
    return current


def apply_heads(query, weights):
    gate_q = jnp.einsum("nhd,hde->nhe", query, weights[:, 0], preferred_element_type=jnp.float32)
    up_q = jnp.einsum("nhd,hde->nhe", query, weights[:, 1], preferred_element_type=jnp.float32)
    hidden_q = (jax.nn.silu(gate_q) * up_q).astype(jnp.bfloat16)
    return jnp.einsum("nhd,hde->nhe", hidden_q, weights[:, 2], preferred_element_type=jnp.float32)


def local_grads(key_rows, value_rows, rate, weights):
    gate_k = jnp.einsum("nhd,hde->nhe", key_rows, weights[:, 0], preferred_element_type=jnp.float32)
    up_k = jnp.einsum("nhd,hde->nhe", key_rows, weights[:, 1], preferred_element_type=jnp.float32)
    sig = jax.nn.sigmoid(gate_k)
    hidden = (gate_k * sig * up_k).astype(jnp.bfloat16)
    scaled = (rate.T[:, :, None] * value_rows.astype(jnp.float32)).astype(jnp.bfloat16)
    back = jnp.einsum("nhe,hde->nhd", scaled, weights[:, 2], preferred_element_type=jnp.float32)
    grad_gate = (back * up_k * sig * (1.0 + gate_k * (1.0 - sig))).astype(jnp.bfloat16)
    grad_up = (back * gate_k * sig).astype(jnp.bfloat16)
    g_gate = jnp.einsum("nhd,nhe->hde", key_rows, grad_gate, preferred_element_type=jnp.float32)
    g_up = jnp.einsum("nhd,nhe->hde", key_rows, grad_up, preferred_element_type=jnp.float32)
    g_down = jnp.einsum("nhd,nhe->hde", hidden, scaled, preferred_element_type=jnp.float32)
    return jnp.stack([g_gate, g_up, g_down], axis=1)


def finish(joined, totals, out_gain):
    return (joined / jnp.sqrt(totals[:, None] / D + 1e-06) * out_gain[None, :]).astype(jnp.bfloat16)


def per_device(queries, keys, values, rates, fast_init, out_gain):
    heads_here = fast_init.shape[0]
    head_size = fast_init.shape[2]
    tok_rows = queries.shape[1]
    weights = fast_init
    outputs = []
    joined_all = []
    for block in range(queries.shape[0]):
        query = queries[block].reshape(tok_rows, heads_here, head_size)
        key_rows = keys[block].reshape(tok_rows, heads_here, head_size)
        value_rows = values[block].reshape(tok_rows, heads_here, head_size)
        joined = apply_heads(query, weights).reshape(tok_rows, heads_here * head_size)
        grads = local_grads(key_rows, value_rows, rates[block], weights)
        total = lax.psum(grads, "tokens")
        squares = jnp.sum(total * total, axis=(2, 3))
        start = (total / (jnp.sqrt(squares)[:, :, None, None] + 1e-07)).astype(jnp.bfloat16)
        update = newton(start)
        weights = (weights.astype(jnp.float32) + step_size * update.astype(jnp.float32)).astype(
            jnp.bfloat16
        )
        joined_all.append(joined)
    stacked = jnp.stack(joined_all, axis=0)
    totals = lax.psum(jnp.sum(stacked * stacked, axis=2), "heads")
    outputs = [
        finish(joined_all[index], totals[index], out_gain) for index in range(len(joined_all))
    ]
    return (jnp.stack(outputs, axis=0), weights)


F32 = jnp.float32
BF16 = jnp.bfloat16
MESH = pl.DeviceIdType.MESH
DOWN, GATE, UP = 2, 0, 1
ORDER = (DOWN, GATE, UP)


def mm(a, b):
    return jnp.dot(a, b, preferred_element_type=F32)


def mm_nt(a, b):
    return lax.dot_general(a, b, (((1,), (1,)), ((), ())), preferred_element_type=F32)


def mm_tn(a, b):
    return lax.dot_general(a, b, (((0,), (0,)), ((), ())), preferred_element_type=F32)


def orthogonalize(mats):
    xs = []
    for g in mats:
        g = g.astype(F32)
        square = jnp.sum(jnp.sum(g * g, axis=1, keepdims=True), axis=0, keepdims=True)
        xs.append((g * (1.0 / (jnp.sqrt(square) + 1e-07))).astype(BF16))
    for _ in range(NS_STEPS):
        grams = [mm_nt(x, x).astype(BF16) for x in xs]
        mixers = [(coef_b * a.astype(F32) + coef_c * mm(a, a)).astype(BF16) for a in grams]
        xs = [(coef_a * x.astype(F32) + mm(b, x)).astype(BF16) for b, x in zip(mixers, xs)]
    return xs


def kernel(
    sizes, q_hbm, k_hbm, v_hbm, r_hbm, w_hbm, gain_hbm, mixed, wout,
    q0, keys0, vals, w0, rates, gain, dps, kv, qb, act, dgu, hid, w_own, w1, wgu, gd_s, gd_r, gg_s, gg_r, full_d, full_g,
    ysend, ybuf, y0, sq, sqr,
    loc_sem, a2a_s, kv_r, late_r, q_r, w_sem, fwd_s, x_s, x_r, c_s, c_r, y_sem, sq_s, sq_r, dist_r, dist_s,
):
    cores, HL, rows, DH = sizes
    width = HL * DH
    half = DH // 2
    core = lax.axis_index("heads")
    t = lax.axis_index("tokens")
    x, y, zl, zh = t % 2, (t // 2) % 2, (t // 4) % 2, t // 8
    z = t // 4
    kind = (x + y + zl) % 2
    home = core == kind
    away = core != kind

    own_slot = x + 2 * y + 4 * zl
    own_head = x + 2 * zl
    mate = t + 8 * (1 - 2 * zh)
    x_near = t + 1 - 2 * x
    y_near = t + 2 * (1 - 2 * y)
    z_near = t + 4 * (1 - 2 * zl)

    def slot(k):
        return (x + k % 2) % 2 + 2 * ((y + k // 2 % 2) % 2) + 4 * ((zl + k // 4) % 2)

    def head_at(dx, dz):
        return (x + dx) % 2 + 2 * ((zl + dz) % 2)

    def owner(dx, dz):
        x0, z0 = (x + dx) % 2, (zl + dz) % 2
        return x0 + 2 * ((x0 + z0 + core) % 2) + 4 * z0 + 8 * zh

    def remote(src, dst, send_sem, recv_sem, device):
        return pltpu.make_async_remote_copy(
            src_ref=src, dst_ref=dst, send_sem=send_sem, recv_sem=recv_sem,
            device_id=device, device_id_type=MESH,
        )

    def send(src, dst, send_sem, recv_sem, device):
        remote(src, dst, send_sem, recv_sem, device).start()

    def arrived(ref, recv_sem):
        remote(ref, ref, loc_sem.at[0], recv_sem, {"tokens": x_near}).wait_recv()

    def drained(ref, send_sem):
        remote(ref, ref, send_sem, loc_sem.at[0], {"tokens": x_near}).wait_send()

    def cols(h):
        return pl.ds(pl.multiple_of(h * DH, DH), DH)

    twin = {"heads": 1 - core}

    local_v = [pltpu.make_async_copy(v_hbm.at[b], vals.at[b], loc_sem.at[4 + b]) for b in range(2)]
    local_r = pltpu.make_async_copy(r_hbm, rates, loc_sem.at[2])
    local_q = pltpu.make_async_copy(q_hbm.at[0], q0, loc_sem.at[0])
    local_w = pltpu.make_async_copy(w_hbm, w0, loc_sem.at[1])
    local_gain = pltpu.make_async_copy(gain_hbm, gain, loc_sem.at[3])
    own_w = pltpu.make_async_copy(w_hbm.at[own_head], w_own, w_sem.at[0])
    local_k = pltpu.make_async_copy(k_hbm.at[0], keys0, loc_sem.at[6])
    local_k.start()
    local_r.start()
    local_v[0].start()
    barrier = pltpu.get_barrier_semaphore()

    @pl.when(away)
    def _():
        for k in range(8):
            pl.semaphore_signal(
                barrier, inc=1, device_id={"heads": 1 - core, "tokens": slot(k) + 8 * zh}, device_id_type=MESH
            )

    for device in ({"heads": 1 - core}, *({"tokens": chip} for chip in (mate, x_near, y_near, z_near))):
        pl.semaphore_signal(barrier, inc=1, device_id=device, device_id_type=MESH)
    local_w.start()
    local_q.start()
    local_v[1].start()
    local_gain.start()

    @pl.when(home)
    def _():
        own_w.start()

    pl.semaphore_wait(barrier, HL + 5)

    def spread(array, view, landing, recv_sems, both=False):
        for dx, dz in SPREAD:
            send(view(head_at(dx, dz)), landing.at[own_slot], a2a_s.at[array], recv_sems(own_slot),
                 {"heads": core if both and dz else 1 - core, "tokens": owner(dx, dz)})

    def landed(array):
        return lambda i: kv_r.at[array, i] if array < 2 else late_r.at[array - 2]

    def spread_keys(b):
        spread(2 * b, lambda j: (k_hbm.at[b, :, cols(j)] if b else keys0.at[:, cols(j)]), kv.at[2 * b], landed(2 * b))

    def spread_values(b):
        spread(2 * b + 1, lambda j: dps.at[b, j], kv.at[2 * b + 1], landed(2 * b + 1))

    def spread_queries():
        spread(4, lambda j: q_hbm.at[1, :, cols(j)], qb, lambda i: q_r.at[0], both=True)

    def scale_values(b):
        for j in range(HL):
            rate = jnp.broadcast_to(rates[b, pl.ds(j, 1), :], (rows, rows)).T[:, :1]
            dps[b, j] = (rate * vals[b, :, j * DH:(j + 1) * DH].astype(F32)).astype(BF16)

    def issue(point):
        for when, what in zip(ISSUE, (lambda: spread_keys(1), lambda: spread_values(1), spread_queries)):
            if when == point:
                what()

    local_k.wait()
    spread_keys(0)

    @pl.when(home)
    def _():
        send(w_hbm.at[own_head], w_own, fwd_s.at[5], w_sem.at[0], twin)

    local_r.wait()
    local_v[0].wait()
    scale_values(0)
    spread_values(0)
    local_v[1].wait()
    scale_values(1)

    def share_squares(b, square):
        sq[b] = jnp.broadcast_to(square, (rows, 128))
        send(sq.at[b], sqr.at[b], sq_s.at[b], sq_r.at[b], twin)

    def finish_block(b, read):
        total = sq[b]
        arrived(sqr.at[b], sq_r.at[b])
        total = total + sqr[b]
        root = jnp.sqrt(total[:, :1] / (cores * width) + 1e-06)
        for h in range(HL):
            span = slice(h * DH, (h + 1) * DH)
            mixed[b, :, span] = (read(h) / root * gain[:, span]).astype(BF16)

    def fast_net(rows_in, w_gate, w_up, w_down):
        gate = mm(rows_in, w_gate)
        hidden = (jax.nn.silu(gate) * mm(rows_in, w_up)).astype(BF16)
        return mm(hidden, w_down)

    local_w.wait()
    local_q.wait()
    square = jnp.zeros((rows, 1), F32)
    for h in range(HL):
        span = slice(h * DH, (h + 1) * DH)
        out = fast_net(q0[:, span], w0[h, 0], w0[h, 1], w0[h, 2])
        y0[:, span] = out
        square = square + jnp.sum(out * out, axis=1, keepdims=True)
    share_squares(0, square)

    def halve_weights(w):
        for c in range(2):
            span = slice(c * half, (c + 1) * half)
            wgu[c] = jnp.concatenate([w[GATE, :, span], w[UP, :, span]], axis=1)

    def forward(array, i, when):
        @pl.when(when)
        def _():
            send(kv.at[array, i], kv.at[array, i], fwd_s.at[array], kv_r.at[array, i], twin)

    def gradients(b, w):
        weights = wgu[core]
        w_down = w[DOWN, pl.ds(pl.multiple_of(core * half, half), half), :]
        def activations(i, gate_up, back):
            gate = gate_up[:, :half]
            up = gate_up[:, half:]
            sig = jax.nn.sigmoid(gate)
            hid[i] = (gate * sig * up).astype(BF16)
            dgu[i, :, :half] = (back * up * sig * (1.0 + gate * (1.0 - sig))).astype(BF16)
            dgu[i, :, half:] = (back * gate * sig).astype(BF16)

        if b == 0:
            for n, k in enumerate(WAITS):
                i = slot(k)
                arrived(kv.at[0, i], kv_r.at[0, i])
                forward(0, i, away)
                act[k] = mm(kv[0, i], weights)
                issue(10 + n)
            for n, k in enumerate(WAITS):
                i = slot(k)
                arrived(kv.at[1, i], kv_r.at[1, i])
                forward(1, i, away)
                activations(i, act[k], mm_nt(kv[1, i], w_down))
                issue(20 + n)
        else:
            @pl.when(home)
            def _():
                arrived(kv.at[2], late_r.at[0])
                arrived(kv.at[3], late_r.at[1])

            for i in range(8):
                activations(i, mm(kv[2, i], weights), mm_nt(kv[3, i], w_down))
        count = 8 * rows
        grad = mm_tn(hid[...].reshape(count, half), kv[2 * b + 1].reshape(count, DH))
        gd_s[b] = grad.astype(BF16)
        send(gd_s.at[b], gd_r.at[b], x_s.at[b], x_r.at[b, DOWN], {"tokens": mate})
        grad = mm_tn(kv[2 * b].reshape(count, DH), dgu[...].reshape(count, DH)).astype(BF16)
        gg_s[b, GATE] = grad[:, :half]
        send(gg_s.at[b, GATE], gg_r.at[b, GATE], x_s.at[b], x_r.at[b, GATE], {"tokens": mate})
        gg_s[b, UP] = grad[:, half:]
        send(gg_s.at[b, UP], gg_r.at[b, UP], x_s.at[b], x_r.at[b, UP], {"tokens": mate})

    def exchange(b, m):
        if m == DOWN:
            mine, theirs, full = gd_s.at[b], gd_r.at[b], full_d
        else:
            mine, theirs, full = gg_s.at[b, m], gg_r.at[b, m], full_g.at[m]
        arrived(theirs, x_r.at[b, m])
        total = (mine[...].astype(F32) + theirs[...].astype(F32)).astype(BF16)
        full[b, core] = total
        here = full.at[b, core]
        if b == 0:
            send(here, here, c_s.at[b], c_r.at[b, m], twin)
        else:
            @pl.when(away)
            def _():
                send(here, here, c_s.at[b], c_r.at[b, m], twin)

    def whole(b, m):
        full = full_d if m == DOWN else full_g.at[m]
        arrived(full.at[b, 1 - core], c_r.at[b, m])
        if m == DOWN:
            return full_d[b].reshape(DH, DH)
        return jnp.concatenate([full_g[m, b, 0], full_g[m, b, 1]], axis=1)

    @pl.when(home)
    def _():
        own_w.wait()

    @pl.when(away)
    def _():
        arrived(w_own, w_sem.at[0])

    halve_weights(w_own)
    gradients(0, w_own)
    local_gain.wait()
    finish_block(0, lambda h: y0[:, h * DH:(h + 1) * DH])
    for n, m in enumerate(ORDER):
        exchange(0, m)
        issue(30 + n)

    def pass_on(array):
        @pl.when(away)
        def _():
            arrived(kv.at[array], late_r.at[array - 2])
            send(kv.at[array], kv.at[array], fwd_s.at[array], late_r.at[array - 2], twin)

    if PASS_EARLY >= 1:
        pass_on(2)
    if PASS_EARLY >= 2:
        pass_on(3)
    updates = orthogonalize([whole(0, m) for m in ORDER])
    if PASS_EARLY < 1:
        pass_on(2)
    if PASS_EARLY < 2:
        pass_on(3)
    for m, update in zip(ORDER, updates):
        w1[m] = (w_own[m].astype(F32) + step_size * update.astype(F32)).astype(BF16)
    halve_weights(w1)
    gradients(1, w1)

    def slot_of(k):
        return (own_slot + 4 * home.astype(jnp.int32)) // 4 % 2 * 4 + k

    def new_outputs(first, last):
        if first < last:
            arrived(qb.at[pl.ds(0, 4)], q_r.at[0])
        for k in range(first, last):
            i = slot_of(k)
            ysend[k] = fast_net(qb[i], w1[GATE], w1[UP], w1[DOWN]).astype(BF16)
            send(ysend.at[k], ybuf.at[own_head], y_sem.at[0], y_sem.at[1], {"heads": kind, "tokens": i + 8 * zh})

    def squares_of_block1():
        arrived(ybuf, y_sem.at[1])
        square = jnp.zeros((rows, 1), F32)
        for h in range(HL):
            out = ybuf[h].astype(F32)
            square = square + jnp.sum(out * out, axis=1, keepdims=True)
        share_squares(1, square)

    def rows_of(j, m, which):
        return wout.at[j, m, pl.ds(which * half, half)]

    def wait_part(j, m, which):
        arrived(rows_of(j, m, which), dist_r.at[j, m, which])

    def pass_part(j, m, which, device):
        part = rows_of(j, m, which)
        send(part, part, dist_s.at[0], dist_r.at[j, m, which], {"tokens": device})

    def start_spread(m):
        for which in range(2):
            for chip in (x_near, y_near, z_near):
                pass_part(own_head, m, which, chip)

    def last_step(m):
        @pl.when(home)
        def _():
            (update,) = orthogonalize([whole(1, m)])
            wout[own_head, m] = (w1[m].astype(F32) + step_size * update.astype(F32)).astype(BF16)
            start_spread(m)

    for n, m in enumerate(ORDER):
        new_outputs(CUTS[n], CUTS[n + 1])
        exchange(1, m)
        last_step(m)
    new_outputs(CUTS[3], 4)

    by_x, by_y, by_z = head_at(1, 0), head_at(0, 0), head_at(0, 1)
    opposite = head_at(1, 1)

    def relay(j, m, chip):
        for which in range(2):
            wait_part(j, m, which)
            pass_part(j, m, which, chip)

    @pl.when(away)
    def _():
        first, second, third = ORDER
        relay(by_z, first, y_near)
        relay(by_x, second, z_near)
        relay(by_x, first, z_near)
        relay(by_y, first, x_near)
        squares_of_block1()
        relay(by_y, third, x_near)
        relay(by_y, second, x_near)
        relay(by_z, second, y_near)
        relay(by_x, third, z_near)
        relay(by_z, third, y_near)

    relays = ((by_z, x_near), (opposite, y_near), (by_x, z_near))

    @pl.when(home)
    def _():
        for n, (m, (j, chip)) in enumerate(zip(ORDER, relays)):
            if n == 2:
                squares_of_block1()
            relay(j, m, chip)

    finish_block(1, lambda h: ybuf[h].astype(F32))

    @pl.when(away)
    def _():
        for m in ORDER:
            for which in range(2):
                wait_part(opposite, m, which)

    @pl.when(home)
    def _():
        for m, (relayed, _) in zip(ORDER, relays):
            for j, _ in relays:
                if j is not relayed:
                    for which in range(2):
                        wait_part(j, m, which)

    drained(wout.at[pl.ds(0, 3)], dist_s.at[0])

    @pl.when(home)
    def _():
        drained(wout.at[0], dist_s.at[0])

    for i in range(5):
        drained(qb.at[pl.ds(0, HL)], a2a_s.at[i])

    @pl.when(away)
    def _():
        for i in range(4):
            drained(qb, fwd_s.at[i])
        drained(full_d.at[0], c_s.at[1])
        drained(full_d.at[0, 0], c_s.at[1])

    @pl.when(home)
    def _():
        drained(w_own, fwd_s.at[5])

    for b in range(2):
        drained(full_d.at[0], x_s.at[b])
        drained(full_d.at[0, 0], x_s.at[b])
        drained(sqr.at[b], sq_s.at[b])
    drained(full_d.at[0], c_s.at[0])
    drained(full_d.at[0, 0], c_s.at[0])
    drained(ysend, y_sem.at[0])


WAITS = (0, 7, 3, 5, 6, 1, 2, 4)
SPREAD = ((1, 1), (0, 1), (1, 0), (0, 0))
ISSUE = (10, 23, 32)
PASS_EARLY = 2
CUTS = (0, 4, 4, 4)


def one_kernel(cores, queries, keys, values, rates, fast_init, out_gain):
    blocks, rows, width = queries.shape
    HL, _, DH, _ = fast_init.shape
    half = DH // 2
    dma = lambda *shape: pltpu.SemaphoreType.DMA(shape)
    vm = pltpu.VMEM
    any_space = pl.BlockSpec(memory_space=pl.ANY)
    in_vmem = pl.BlockSpec(memory_space=pltpu.VMEM)
    results = pl.pallas_call(
        functools.partial(kernel, (cores, HL, rows, DH)),
        out_shape=(pltpu.VMEM(queries.shape, BF16), pltpu.VMEM(fast_init.shape, BF16)),
        in_specs=[any_space] * 6,
        out_specs=(in_vmem, in_vmem),
        scratch_shapes=[
            vm((rows, width), BF16),
            vm((rows, width), BF16),
            vm((2, rows, width), BF16),
            vm(fast_init.shape, BF16),
            vm(rates.shape, F32),
            vm((1, width), F32),
            vm((2, HL, rows, DH), BF16),
            vm((4, 8, rows, DH), BF16),
            vm((8, rows, DH), BF16),
            vm((8, rows, DH), F32),
            vm((8, rows, DH), BF16),
            vm((8, rows, half), BF16),
            vm((3, DH, DH), BF16),
            vm((3, DH, DH), BF16),
            vm((2, DH, DH), BF16),
            vm((2, half, DH), BF16),
            vm((2, half, DH), BF16),
            vm((2, 2, DH, half), BF16),
            vm((2, 2, DH, half), BF16),
            vm((2, 2, half, DH), BF16),
            vm((2, 2, 2, DH, half), BF16),
            vm((HL, rows, DH), BF16),
            vm((HL, rows, DH), BF16),
            vm((rows, width), F32),
            vm((2, rows, 128), F32),
            vm((2, rows, 128), F32),
            dma(7),
            dma(5), dma(2, 8), dma(2), dma(1), dma(1), dma(6),
            dma(2), dma(2, 3), dma(2), dma(2, 3),
            dma(2), dma(2), dma(2),
            dma(4, 3, 2), dma(1),
        ],
        compiler_params=pltpu.CompilerParams(collective_id=0, has_side_effects=True),
    )(queries, keys, values, rates, fast_init, out_gain.reshape(1, width))
    return store(*results)


def store_kernel(mixed, weights, mixed_out, weights_out, sems):
    copies = [pltpu.make_async_copy(mixed.at[b], mixed_out.at[b], sems.at[b]) for b in range(2)]
    copies += [pltpu.make_async_copy(weights.at[h], weights_out.at[h], sems.at[2 + h]) for h in range(weights.shape[0])]
    for copy in copies:
        copy.start()
    for copy in copies:
        copy.wait()


def store(mixed, weights):
    return pl.pallas_call(
        store_kernel,
        out_shape=(jax.ShapeDtypeStruct(mixed.shape, BF16), jax.ShapeDtypeStruct(weights.shape, BF16)),
        in_specs=[pl.BlockSpec(memory_space=pl.ANY)] * 2,
        out_specs=(pl.BlockSpec(memory_space=pltpu.HBM), pl.BlockSpec(memory_space=pltpu.HBM)),
        scratch_shapes=[pltpu.SemaphoreType.DMA((2 + weights.shape[0],))],
    )(*(pltpu.with_memory_space_constraint(a, pltpu.VMEM) for a in (mixed, weights)))


def fits(cores, token_devices, queries, fast_init):
    blocks, rows, width = queries.shape
    HL, _, DH, _ = fast_init.shape
    return (
        blocks == 2 and HL == 4 and cores == 2 and token_devices == 16
        and rows == 128 and DH == 256
    )


def per_device_best(cores, token_devices, queries, keys, values, rates, fast_init, out_gain):
    if fits(cores, token_devices, queries, fast_init):
        return one_kernel(cores, queries, keys, values, rates, fast_init, out_gain)
    return per_device(queries, keys, values, rates, fast_init, out_gain)


def solution(mesh):
    in_specs = (
        P(None, "tokens", "heads"),
        P(None, "tokens", "heads"),
        P(None, "tokens", "heads"),
        P(None, "heads", "tokens"),
        P("heads", None, None, None),
        P("heads"),
    )
    out_specs = (P(None, "tokens", "heads"), P("heads", None, None, None))
    return jax.shard_map(
        functools.partial(per_device_best, mesh.shape["heads"], mesh.shape["tokens"]), mesh=mesh, in_specs=in_specs, out_specs=out_specs, check_vma=False
    )
```
